32 devices in a mesh: lat: 4 (over z), lon: 8 (over y, x, core).
Axes of the slice: x: 2, y: 2, z: 4, core: 2. Of those that a mesh axis runs over, the one named last changes fastest.
Arguments:
- lat_coef: float32 [4, 256, 1024], P(None, 'lat', 'lon'), may hold values from 0.02 to 0.12
- lon_coef: float32 [4, 256, 1024], P(None, 'lat', 'lon'), may hold values from 0.02 to 0.12
- std_scale: float32 [4, 256, 1024], P(None, 'lat', 'lon'), may hold values from 0.5 to 2
- land_mask: int32 [256, 1024], P('lat', 'lon'), may hold values 0 or 1
- lst_weights: float32 [4], replicated, may hold values from 0.1 to 0.6
- innovation: float32 [16384, 128], P(('lat', 'lon')), may hold values from -6 to 6
- inv_var: float32 [16384, 128], P(('lat', 'lon')), may hold values from 0.2 to 5
- owner: int32 [16384, 1], P(('lat', 'lon')), may hold values from 0 to 31; in each aligned block of 512 rows (0 to 511, 512 to 1023, ...) at most 32 rows name the same one
- row_ids: int32 [16384], P(('lat', 'lon')), may hold values from 0 to 63
- offsets: int32 [16384, 128], P(('lat', 'lon')), may hold values from 0 to 127
Outputs:
- increment: float32 [4, 256, 1024], P(None, 'lat', 'lon')
- departure: float32 [16384, 128], P(('lat', 'lon'))
The draws below stay inside these ranges and needn't reach their ends.
Inputs may be any that keep to these rules, and one draw needn't show every extreme that they name: Within the 512 tiles of one device no owner is named more than 32 times.
All inputs are finite; a program needn't handle non-finite values. No bound on the sum of `land_mask` on one device may be relied on, other than what follows from the above.
Results may differ from the reference program's by a relative error of at most 0.00026.
Values sent between devices are 32-bit elements; how exact they have to be, the bound alone decides.
No kernel may reach another device: no remote copies, remote signals or barrier semaphores. Data moves between devices by JAX's collectives and lax.ppermute only.
A program may use at most 64 MiB of HBM per device.

```python
import math
import jax
import jax.numpy as jnp
import numpy as np

F = 4
ROW = 128
PASSES = 8
ITERS = 2
CLAT = 64
CLON = 128
TILES_DEV = 512
CAP = 32
ROWS_DEV = 64
NLAT = 256
NLON = 1024
TILES = 16384
N_LON = 8
DEVICES = 32


def set_ends(array, rng, smallest, top_value):
    longest = array.shape.index(max(array.shape))
    spots = []
    for shift in (0, 1):
        where = [jax.random.randint(jax.random.fold_in(rng, axis), (), 0, length) for axis, length in enumerate(array.shape)]
        where[longest] = (where[longest] + shift) % array.shape[longest]
        spots.append(tuple(where))
    return array.at[spots[0]].set(smallest).at[spots[1]].set(top_value)


def block_levels(rng, extent, split, smallest, largest):
    gain = 1.0
    for axis_at, shards_of in split:
        heights = jax.random.uniform(jax.random.fold_in(jax.random.fold_in(rng, 6), axis_at), (shards_of,), jnp.float32, smallest / len(split), largest / len(split))
        gain = gain * jnp.repeat(jnp.exp(heights), extent[axis_at] // shards_of).reshape((-1,) + (1,) * (len(extent) - 1 - axis_at))
    return gain


def routed_block(key, own, number, rows, number_of, top, bound, slope):
    ranking = jax.random.permutation(key, number_of)
    crowded, usual = load_shares(number_of, rows * top, bound, slope, True), load_shares(number_of, rows * top, bound, slope, False)
    places = jnp.arange(number_of)

    def named(lengths, rotation):
        used = int((lengths > 0).sum())
        fixed = max(1, used // 4)
        moved = fixed + (places - fixed + rotation * (used - fixed)) % max(1, number_of - fixed)
        return jnp.zeros((number_of,), jnp.int32).at[ranking[jnp.where(places < fixed, places, moved)]].set(jnp.asarray(lengths, jnp.int32))

    lengths = jnp.where(number % 4 == 0, named(crowded, number // 4), named(usual, number - number // 4 - 1))
    mixed = jax.random.permutation(jax.random.fold_in(own, 3), number_of)
    source_of, receiver = mixed[0:number_of // 2 * 2:2], mixed[1:number_of // 2 * 2:2]
    slack = jnp.minimum(lengths[source_of] - 1, bound - lengths[receiver]) // 2
    slack = jnp.where((source_of == ranking[0]) | (receiver == ranking[0]) | (lengths[receiver] == 0), 0, jnp.maximum(slack, 0))
    moved = jax.random.randint(jax.random.fold_in(own, 4), (number_of // 2,), 0, 1 << 20) % (slack + 1)
    lengths = lengths.at[source_of].add(-moved).at[receiver].add(moved)
    items = jnp.searchsorted(jnp.cumsum(lengths), jnp.arange(rows * top), side="right").astype(jnp.int32)
    listing = items.reshape(top, rows).T
    listing = listing[jax.random.permutation(jax.random.fold_in(own, 1), rows)]
    rotation = jax.random.randint(jax.random.fold_in(own, 2), (rows, 1), 0, top)
    return jnp.take_along_axis(listing, (jnp.arange(top)[None, :] + rotation) % top, axis=1)


def load_shares(amount, total, bound, slope, full):
    loads = [(1 << 20) // math.isqrt(grade ** slope) + 1 for grade in range(1, amount + 1)]
    largest = bound if full else min(bound, max(-(-total // amount), total * loads[0] // sum(loads)))
    least = 1 if total - largest >= amount - 1 else 0
    holding, rest = [largest] + [least] * (amount - 1), total - largest - least * (amount - 1)
    while rest > 0:
        movable = [i for i in range(1, amount) if holding[i] < largest] or [i for i in range(1, amount) if holding[i] < bound]
        mass, budget = sum([loads[i] for i in movable]), rest
        for i in movable:
            more = min(bound - holding[i], max(1, budget * loads[i] // mass), rest)
            holding[i] = holding[i] + more
            rest = rest - more
    return np.array(holding)


def bell_draw(rng, extent, deviation, most, split=(), kind=jnp.bfloat16):
    values = deviation * jax.random.normal(rng, extent, jnp.float32)
    if split:
        values = values * block_levels(rng, extent, split, -0.22, 0.18)
    return jnp.clip(values, -most, most).astype(kind)


def setup_inputs(seed: int = 0) -> dict:
    key_of = jax.random.split(jax.random.key(seed), 11)
    lat_coef = jnp.clip(0.02 + 0.09999999776482582 * jax.random.uniform(key_of[0], (F, NLAT, NLON), jnp.float32) ** block_levels(key_of[0], (F, NLAT, NLON), ((1, 4), (2, 8)), -0.2, 0.2), 0.02, 0.12)
    lon_coef = jnp.clip(0.02 + 0.09999999776482582 * jax.random.uniform(key_of[1], (F, NLAT, NLON), jnp.float32) ** block_levels(key_of[1], (F, NLAT, NLON), ((1, 4), (2, 8)), -0.2, 0.2), 0.02, 0.12)
    std_scale = jnp.clip(jnp.exp(math.log(2.0) - 1.3862944 * jax.random.uniform(key_of[2], (F, NLAT, NLON), jnp.float32) ** block_levels(key_of[2], (F, NLAT, NLON), ((1, 4), (2, 8)), -0.2, 0.2)), 0.5, 2.0)
    land_mask = set_ends((jax.random.randint(key_of[3], (NLAT, NLON), 0, 4) < 3).astype(jnp.int32), jax.random.fold_in(key_of[3], 1), 0, 1)
    lst_weights = jnp.clip(jax.random.uniform(key_of[4], (F,), jnp.float32, 0.1, 0.6), 0.1, 0.6)
    innovation = bell_draw(key_of[5], (TILES, ROW), 1.0, 6.0, ((0, 32),), jnp.float32)
    inv_var = jnp.clip(jnp.exp(math.log(5.0) - 3.218876 * jax.random.uniform(key_of[6], (TILES, ROW), jnp.float32) ** block_levels(key_of[6], (TILES, ROW), ((0, 32),), -0.2, 0.2)), 0.2, 5.0)
    owner_keys = jax.random.split(jax.random.fold_in(key_of[7], 1), TILES // TILES_DEV)
    owner_turns = jax.random.permutation(jax.random.fold_in(key_of[7], 3), TILES // TILES_DEV)
    owner = jax.vmap(lambda own, number: routed_block(jax.random.fold_in(key_of[7], 2), own, number, TILES_DEV, DEVICES, 1, CAP, 2))(owner_keys, owner_turns).reshape((TILES, 1))
    row_ids = set_ends(jax.random.randint(key_of[8], (TILES,), 0, ROWS_DEV), jax.random.fold_in(key_of[8], 1), 0, ROWS_DEV - 1).astype(jnp.int32)
    offsets = set_ends(jax.random.randint(key_of[9], (TILES, ROW), 0, ROW), jax.random.fold_in(key_of[9], 1), 0, ROW - 1).astype(jnp.int32)
    return {"lat_coef": lat_coef, "lon_coef": lon_coef, "std_scale": std_scale, "land_mask": land_mask, "lst_weights": lst_weights, "innovation": innovation, "inv_var": inv_var, "owner": owner, "row_ids": row_ids, "offsets": offsets}


def lst_of(weights, field):
    total = weights[0] * field[0]
    for index in range(1, field.shape[0]):
        total = total + weights[index] * field[index]
    return total


def diffuse(field, north_face, east_face):
    south_face = jnp.roll(north_face, 1, axis=1)
    west_face = jnp.roll(east_face, 1, axis=2)
    for index in range(PASSES):
        north = jnp.roll(field, -1, axis=1)
        south = jnp.roll(field, 1, axis=1)
        east = jnp.roll(field, -1, axis=2)
        west = jnp.roll(field, 1, axis=2)
        field = field + north_face * (north - field) - south_face * (field - south) + east_face * (east - field) - west_face * (field - west)
    return field


def reference(lat_coef, lon_coef, std_scale, land_mask, lst_weights, innovation, inv_var, owner, row_ids, offsets):
    north_face = lat_coef.at[:, -1, :].set(0.0)
    mask_field = land_mask.astype(jnp.float32)
    owner_flat = owner[:, 0]
    cells = row_ids[:, None] * ROW + offsets
    glat = (owner_flat // N_LON)[:, None] * CLAT + cells // CLON
    glon = (owner_flat % N_LON)[:, None] * CLON + cells % CLON

    def forward(vector):
        return mask_field * std_scale * diffuse(vector, north_face, lon_coef)

    def adjoint(vector):
        return diffuse(mask_field * std_scale * vector, north_face, lon_coef)

    def observe(field):
        return lst_of(lst_weights, field)[glat, glon]

    def spread_back(values):
        grid = jnp.zeros((NLAT, NLON), jnp.float32).at[glat, glon].add(values)
        return lst_weights[:, None, None] * grid[None]

    residual = adjoint(spread_back(inv_var * innovation))
    direction = residual
    norm_now = jnp.sum(residual * residual)
    increment = jnp.zeros_like(residual)
    analysed = jnp.zeros_like(innovation)
    for index in range(ITERS):
        image = forward(direction)
        seen = observe(image)
        product = direction + adjoint(spread_back(inv_var * seen))
        step_size = norm_now / jnp.sum(direction * product)
        increment = increment + step_size * image
        analysed = analysed + step_size * seen
        if index + 1 < ITERS:
            residual = residual - step_size * product
            norm_next = jnp.sum(residual * residual)
            direction = residual + (norm_next / norm_now) * direction
            norm_now = norm_next
    return increment, innovation - analysed
```

```python
import functools

import jax
import jax.numpy as jnp
from jax import lax
from jax.experimental import pallas as pl
from jax.experimental.pallas import tpu as pltpu
from jax.sharding import PartitionSpec as P

PASSES = 8
RIM = 4 * PASSES
LANES = 128
SUB = 8
GROUP = 8
LOW = 32
AXES = ("lat", "lon")
F32 = jnp.float32
BF16 = jnp.bfloat16


def iota(shape, dim):
    return lax.broadcasted_iota(jnp.int32, shape, dim)


def call(kernel, outs, args, scratch=(), smem=(), flops=1000, nbytes=100000):
    vmem = pl.BlockSpec(memory_space=pltpu.VMEM)
    smem_spec = pl.BlockSpec(memory_space=pltpu.SMEM)
    return pl.pallas_call(
        kernel,
        out_shape=[jax.ShapeDtypeStruct(shape, dtype) for shape, dtype in outs],
        in_specs=[smem_spec if index in smem else vmem for index in range(len(args))],
        out_specs=[vmem] * len(outs),
        scratch_shapes=list(scratch),
        cost_estimate=pl.CostEstimate(flops=flops, bytes_accessed=nbytes, transcendentals=0),
    )(*args)


def split(value):
    high = value.astype(BF16)
    low = (value - high.astype(F32)).astype(BF16)
    return high, low


def contract(left, right, dims):
    return lax.dot_general(left, right, (dims, ((), ())), preferred_element_type=F32)


def swap_blocks(x, sub, lane):
    block = lane // LOW
    own = sub % 4
    up = pltpu.roll(pltpu.roll(x, SUB - 1, 0), LOW, 1)
    down = pltpu.roll(pltpu.roll(x, 1, 0), LANES - LOW, 1)
    odd_row, odd_block = own % 2, block % 2
    x = jnp.where(odd_row == odd_block, x, jnp.where(odd_row == 0, up, down))
    turned = pltpu.roll(x, 2 * LOW, 1)
    up = pltpu.roll(turned, SUB - 2, 0)
    down = pltpu.roll(turned, 2, 0)
    high_row, high_block = own // 2, block // 2
    return jnp.where(high_row == high_block, x, jnp.where(high_row == 0, up, down))


def route_kernel(devices, capacity, owner_ref, rid_ref, me_ref, inn_ref, var_ref, off_ref, send_ref, slot_ref, rows_ref):
    tiles = off_ref.shape[0]
    per_row = LANES // capacity
    hits = (owner_ref[...] == iota((tiles, LANES), 1)).astype(F32)
    earlier = (iota((tiles, tiles), 1) < iota((tiles, tiles), 0)).astype(BF16)
    before = jnp.dot(earlier, hits.astype(BF16), preferred_element_type=F32)
    rank = jnp.sum(hits * before, axis=1, keepdims=True)
    slot = owner_ref[...].astype(F32) * capacity + rank
    slot_wide = jnp.broadcast_to(slot, (tiles, LANES))
    slot_ref[...] = slot_wide
    slot_row = jnp.transpose(slot_wide)[0:1, :].astype(jnp.int32)
    shift = (me_ref[0] % per_row) * capacity
    rank_hot = (rank.astype(jnp.int32) + shift == iota((tiles, LANES), 1)).astype(BF16)
    marked = jnp.transpose(hits) * (rid_ref[...].astype(F32) + 1.0)
    ids = jnp.dot(marked.astype(BF16), rank_hot, preferred_element_type=F32)
    spare = send_ref.shape[1] - 2 * capacity
    pad_row = iota((devices, spare, LANES), 1)
    send_ref[:, 2 * capacity :, :] = jnp.where(
        pad_row == 0, jnp.broadcast_to(ids[0:devices][:, None, :], (devices, spare, LANES)), 0.0
    )

    sub = iota((SUB, LANES), 0)
    lane = iota((SUB, LANES), 1)
    tall = iota((LOW, LANES), 0)

    def expand(index, carry):
        start = pl.multiple_of(index * GROUP, GROUP)
        window = pl.ds(start, GROUP)
        offsets = off_ref[window, :]
        weight = var_ref[window, :]
        value = weight * inn_ref[window, :]
        low = offsets % LOW
        high = offsets // LOW
        hot, parts = [], []
        for tile in range(GROUP):
            pick = slice(tile, tile + 1)
            hot.append((low[pick, :] == tall).astype(F32).astype(BF16))
            both = jnp.where(sub < 4, value[pick, :], weight[pick, :])
            parts.append(jnp.where(high[pick, :] == sub % 4, both, 0.0))
        upper, lower = split(jnp.concatenate(parts, 0))
        product = contract(jnp.concatenate([upper, lower], 0), jnp.concatenate(hot, 0), ((1,), (1,)))
        half = GROUP * SUB
        total = product[:half] + product[half:]
        quads = []
        for side in range(2):
            lanes = slice(side * LANES, (side + 1) * LANES)
            merged = total[side * 4 * SUB : (side * 4 + 1) * SUB, lanes]
            for tile in range(1, 4):
                base = (side * 4 + tile) * SUB
                merged = jnp.where(lane // LOW == tile, total[base : base + SUB, lanes], merged)
            quads.append(swap_blocks(merged, sub, lane))
        first, second = quads
        rows_ref[window, 0:LANES] = jnp.where(sub < 4, first, pltpu.roll(second, 4, 0))
        rows_ref[window, LANES : 2 * LANES] = jnp.where(sub < 4, pltpu.roll(first, 4, 0), second)
        return carry

    lax.fori_loop(0, tiles // GROUP, expand, 0, unroll=2)
    upper, lower = split(rows_ref[...])
    for block in range(devices * capacity // LANES):
        place = (iota((LANES, tiles), 0) + block * LANES == slot_row).astype(F32).astype(BF16)
        packed = jnp.dot(place, upper, preferred_element_type=F32) + jnp.dot(
            place, lower, preferred_element_type=F32
        )
        owners = slice(block * per_row, (block + 1) * per_row)
        send_ref[owners, 0:capacity, :] = packed[:, 0:LANES].reshape(per_row, capacity, LANES)
        send_ref[owners, capacity : 2 * capacity, :] = packed[:, LANES:].reshape(per_row, capacity, LANES)


def collect_kernel(capacity, got_ref, low_ref, high_ref, ids_ref):
    devices = got_ref.shape[0]
    per_row = LANES // capacity
    rows = 2 * low_ref.shape[1]
    total = jnp.zeros((rows, 2 * LANES), F32)
    tall = iota((rows, LANES), 0) + 1
    for block in range(devices // per_row):
        owners = slice(block * per_row, (block + 1) * per_row)
        ids = jnp.sum(got_ref[owners, 2 * capacity : 2 * capacity + SUB, :], axis=0)[0:1, :]
        ids_ref[block : block + 1, :] = ids
        hot = (ids.astype(jnp.int32) == tall).astype(F32).astype(BF16)
        values = jnp.concatenate(
            [
                got_ref[owners, 0:capacity, :].reshape(LANES, LANES),
                got_ref[owners, capacity : 2 * capacity, :].reshape(LANES, LANES),
            ],
            1,
        )
        upper, lower = split(values)
        total = total + contract(
            jnp.concatenate([hot, hot], 1), jnp.concatenate([upper, lower], 0), ((1,), (0,))
        )
    half = rows // 2
    for plane in range(2):
        lanes = slice(plane * LANES, (plane + 1) * LANES)
        low_ref[plane] = total[0:half, lanes]
        high_ref[plane] = total[half:, lanes]


def faces_kernel(last_ref, lat_ref, lon_ref, std_ref, mask_ref, low_ref, high_ref):
    fields, rows, cols = lat_ref.shape
    half = rows // 2
    mask = mask_ref[...].astype(F32)
    edge = (iota((rows, cols), 0) == rows - 1) & (last_ref[0] == 1)
    for field in range(fields):
        planes = (jnp.where(edge, 0.0, lat_ref[field]), lon_ref[field], mask * std_ref[field])
        for kind, plane in enumerate(planes):
            low_ref[kind * fields + field] = plane[0:half]
            high_ref[kind * fields + field] = plane[half:]


def turn_kernel(low_ref, high_ref, south_ref, north_ref, mid_ref, first_ref, last_ref):
    for plane in range(low_ref.shape[0]):
        tall = jnp.concatenate([south_ref[plane], low_ref[plane], high_ref[plane], north_ref[plane]], 0)
        turned = jnp.transpose(tall)
        mid_ref[plane] = turned
        first_ref[plane] = turned[0:RIM]
        last_ref[plane] = turned[turned.shape[0] - RIM :]


def weave_kernel(fields, mid_ref, west_ref, east_ref, north_ref, east_face_ref, scale_ref):
    cols = mid_ref.shape[1]
    span = cols // 2 + RIM
    for kind, target in enumerate((north_ref, east_face_ref, scale_ref)):
        for field in range(fields):
            plane = kind * fields + field
            target[pl.ds(field, RIM, stride=SUB), :] = west_ref[plane]
            target[pl.ds(RIM * SUB + field, span, stride=SUB), :] = mid_ref[plane, 0:span, :]
            target[pl.ds(fields + field, span, stride=SUB), :] = mid_ref[plane, cols - span : cols, :]
            target[pl.ds(span * SUB + fields + field, RIM, stride=SUB), :] = east_ref[plane]


def solve_kernel(
    fields,
    north_ref,
    east_ref,
    scale_ref,
    mid_ref,
    west_ref,
    far_ref,
    lam_ref,
    image_ref,
    image_next_ref,
    seen_ref,
    seen_next_ref,
    parts_ref,
    u_ref,
    grid_ref,
    rhs_ref,
    turn_ref,
    t_ref,
):
    cols = mid_ref.shape[1]
    half = cols // 2
    length = half + 2 * RIM
    lam = lam_ref[...]
    sub = iota((SUB, LANES), 0)
    lane = iota((SUB, LANES), 1)
    inner = ((lane >= RIM) & (lane < LANES - RIM)).astype(F32)
    for plane in range(2):
        grid_ref[plane, 0:RIM, :] = west_ref[plane]
        grid_ref[plane, RIM : RIM + cols, :] = mid_ref[plane]
        grid_ref[plane, RIM + cols :, :] = far_ref[plane]

    def at(j):
        return slice(j * SUB, (j + 1) * SUB)

    def grid(plane, j):
        return jnp.where(
            sub < fields, grid_ref[plane, j : j + 1, :], grid_ref[plane, half + j : half + j + 1, :]
        )

    def group_sum(x):
        odd = sub % 2
        x = x + jnp.where(odd == 0, pltpu.roll(x, SUB - 1, 0), pltpu.roll(x, 1, 0))
        top = (sub // 2) % 2
        return x + jnp.where(top == 0, pltpu.roll(x, SUB - 2, 0), pltpu.roll(x, 2, 0))

    def diffuse(edge):
        def one_pass(index, carry):
            low, high = edge + 1, length - edge - 1
            here = u_ref[at(low), :]
            flux = east_ref[at(low - 1), :] * (here - u_ref[at(low - 1), :])
            for j in range(low, high):
                ahead = u_ref[at(j + 1), :]
                flux_next = east_ref[at(j), :] * (ahead - here)
                rise = north_ref[at(j), :] * (pltpu.roll(here, LANES - 1, 1) - here)
                u_ref[at(j), :] = here + ((flux_next - flux) + (rise - pltpu.roll(rise, 1, 1)))
                flux, here = flux_next, ahead
            return carry

        lax.fori_loop(0, PASSES, one_pass, 0)

    first, last = RIM, length - RIM
    for j in range(length):
        u_ref[at(j), :] = lam * scale_ref[at(j), :] * grid(0, j)
    diffuse(0)
    for j in range(first, last):
        rhs_ref[at(j - first), :] = u_ref[at(j), :]
    diffuse(PASSES)
    for j in range(2 * PASSES, length - 2 * PASSES):
        image = scale_ref[at(j), :] * u_ref[at(j), :]
        seen = group_sum(lam * image)
        if first <= j < last:
            image_ref[at(j - first), :] = image
            t_ref[0, at(j - first), :] = seen
        u_ref[at(j), :] = lam * scale_ref[at(j), :] * (grid(1, j) * seen)
    diffuse(2 * PASSES)
    zero = jnp.zeros((SUB, LANES), F32)
    sum_bb, sum_bw = zero, zero
    for j in range(first, last):
        rhs = rhs_ref[at(j - first), :]
        turn = u_ref[at(j), :]
        turn_ref[at(j - first), :] = turn
        sum_bb = sum_bb + rhs * rhs
        sum_bw = sum_bw + rhs * turn
    diffuse(3 * PASSES)
    sum_00, sum_01 = zero, zero
    for j in range(first, last):
        image = scale_ref[at(j), :] * u_ref[at(j), :]
        image_next_ref[at(j - first), :] = image
        seen_next = group_sum(lam * image)
        t_ref[1, at(j - first), :] = seen_next
        seen = t_ref[0, at(j - first), :]
        weighted = grid(1, j) * seen
        sum_00 = sum_00 + weighted * seen
        sum_01 = sum_01 + weighted * seen_next

    def whole(x):
        return jnp.sum(jnp.sum(x * inner, axis=1, keepdims=True), axis=0, keepdims=True)

    def ratio(top, bottom):
        return jnp.where(bottom > 0, top / jnp.where(bottom > 0, bottom, 1.0), 0.0)

    one_of = (sub % fields == 0).astype(F32)
    bb, bw = whole(sum_bb), whole(sum_bw)
    s00, s01 = whole(sum_00 * one_of), whole(sum_01 * one_of)
    fit, seen_fit = ratio(bw, bb), ratio(s01, s00)
    rest, seen_rest = zero, zero
    for j in range(first, last):
        left = turn_ref[at(j - first), :] - fit * rhs_ref[at(j - first), :]
        rest = rest + left * left
        left = t_ref[1, at(j - first), :] - seen_fit * t_ref[0, at(j - first), :]
        seen_rest = seen_rest + grid(1, j) * (left * left)
    rest, seen_rest = whole(rest), whole(seen_rest * one_of)
    wide = iota(parts_ref.shape, 1)
    parts = jnp.zeros(parts_ref.shape, F32)
    for position, number in enumerate((bb, bw, fit, rest, s00, seen_fit, seen_rest)):
        parts = jnp.where(wide == position, number, parts)
    parts_ref[...] = parts
    for plane, target in enumerate((seen_ref, seen_next_ref)):
        flat = jnp.concatenate(
            [
                t_ref[plane, pl.ds(0, half, stride=SUB), :],
                t_ref[plane, pl.ds(fields, half, stride=SUB), :],
            ],
            0,
        )
        target[...] = jnp.transpose(flat)[RIM : LANES - RIM, :]


def answer_kernel(parts_ref, seen_ref, seen_next_ref, ids_ref, back_ref, coef_ref):
    rows = seen_ref.shape[0]

    def column(index):
        return parts_ref[:, index : index + 1]

    def add(x):
        return jnp.sum(x, axis=0, keepdims=True)

    bb_each, fit_each, s00_each, seen_fit_each = column(0), column(2), column(4), column(5)
    bb, bw = add(bb_each), add(column(1))
    fit = bw / bb
    step = bb / (bb + bw)
    gap = fit_each - fit
    rest = add(column(3) + gap * (gap * bb_each))
    tilt = step * rest / bb
    full = fit + tilt
    gap = seen_fit_each - full
    energy = rest + tilt * tilt * bb + add(column(6) + gap * (gap * s00_each))
    step_next = jnp.where(rest > 0, rest / jnp.where(rest > 0, energy, 1.0), 0.0)
    coef = step * (1.0 + step_next * full)
    coef_next = -step * step_next
    final = coef * seen_ref[...] + coef_next * seen_next_ref[...]
    line = iota(coef_ref.shape, 0)
    coef_ref[...] = jnp.where(line == 0, coef, coef_next)
    upper, lower = split(final)
    both = jnp.concatenate([upper, lower], 0)
    blocks = ids_ref.shape[0]
    ids = jnp.transpose(jnp.concatenate([ids_ref[...]] * (LANES // blocks), 0)).astype(jnp.int32)
    wide = iota((LANES, 2 * rows), 1) % rows + 1
    for block in range(blocks):
        hot = (ids[:, block : block + 1] == wide).astype(F32).astype(BF16)
        back_ref[block * LANES : (block + 1) * LANES, :] = jnp.dot(
            hot, both, preferred_element_type=F32
        )


def increment_kernel(fields, image_ref, image_next_ref, coef_ref, out_ref):
    half = image_ref.shape[0] // SUB
    coef, coef_next = coef_ref[0:1, :], coef_ref[1:2, :]
    for field in range(fields):
        parts = []
        for side in range(2):
            pick = pl.ds(side * fields + field, half, stride=SUB)
            parts.append(coef * image_ref[pick, :] + coef_next * image_next_ref[pick, :])
        out_ref[field] = jnp.transpose(jnp.concatenate(parts, 0))[RIM : LANES - RIM, :]


def depart_kernel(back_ref, slot_ref, off_ref, inn_ref, out_ref):
    slots = back_ref.shape[0]
    upper, lower = split(back_ref[...])
    for block in range(off_ref.shape[0] // LANES):
        window = slice(block * LANES, (block + 1) * LANES)
        slot = slot_ref[window, :].astype(jnp.int32)
        place = jnp.concatenate(
            [
                (slot == iota((LANES, LANES), 1) + part * LANES).astype(F32).astype(BF16)
                for part in range(slots // LANES)
            ],
            1,
        )
        rows = jnp.dot(place, upper, preferred_element_type=F32) + jnp.dot(
            place, lower, preferred_element_type=F32
        )
        seen = jnp.take_along_axis(rows, off_ref[window, :], axis=1)
        out_ref[window, :] = inn_ref[window, :] - seen


def neighbours(low, high, axis, periodic):
    count = lax.axis_size(axis)
    forward = [(i, i + 1) for i in range(count - 1)]
    if periodic:
        forward.append((count - 1, 0))
    backward = [(target, source) for source, target in forward]
    return lax.ppermute(high, axis, forward), lax.ppermute(low, axis, backward)


def exchange(low, high):
    planes = low.shape[0]
    south, north = neighbours(low, high, "lat", False)
    mid, first, last = call(
        turn_kernel,
        [((planes, LANES, LANES), F32), ((planes, RIM, LANES), F32), ((planes, RIM, LANES), F32)],
        (low, high, south, north),
        nbytes=4 * planes * 300 * LANES,
    )
    west, east = neighbours(first, last, "lon", True)
    return mid, west, east


def on_device(
    lat_coef, lon_coef, std_scale, land_mask, lst_weights, innovation, inv_var, owner, row_ids, offsets
):
    fields, tile_rows, tile_cols = lat_coef.shape
    tiles, width = innovation.shape
    lat_count, lon_count = lax.axis_size("lat"), lax.axis_size("lon")
    devices = lat_count * lon_count
    capacity = max(2, 2 * tiles // devices)
    if (2 * fields, tile_cols, width, tile_rows + 2 * RIM) != (SUB, LANES, LANES, LANES):
        raise ValueError("tile shape")
    if RIM > tile_rows // 2 or capacity % SUB or LANES % capacity or tiles % LANES:
        raise ValueError("slot shape")
    half = tile_rows // 2
    slots = devices * capacity
    last = (lax.axis_index("lat") == lat_count - 1).astype(jnp.int32).reshape(1)
    me = (lax.axis_index("lat") * lon_count + lax.axis_index("lon")).astype(jnp.int32).reshape(1)

    face_low, face_high = call(
        faces_kernel,
        [((3 * fields, half, LANES), F32)] * 2,
        (last, lat_coef, lon_coef, std_scale, land_mask),
        smem=(0,),
    )
    block = 2 * capacity + SUB
    send, slot = call(
        functools.partial(route_kernel, devices, capacity),
        [((devices, block, LANES), F32), ((tiles, LANES), F32)],
        (owner, row_ids.reshape(1, tiles), me, innovation, inv_var, offsets),
        scratch=(pltpu.VMEM((tiles, 2 * LANES), F32),),
        smem=(2,),
        flops=10**9,
        nbytes=10**7,
    )
    face_mid, face_west, face_east = exchange(face_low, face_high)
    got = lax.all_to_all(send, AXES, split_axis=0, concat_axis=0, tiled=True)
    span = tile_cols // 2 + 2 * RIM
    north8, east8, scale8 = call(
        functools.partial(weave_kernel, fields),
        [((span * SUB, LANES), F32)] * 3,
        (face_mid, face_west, face_east),
        nbytes=3 * 10**6,
    )
    low, high, ids = call(
        functools.partial(collect_kernel, capacity),
        [((2, half, LANES), F32)] * 2 + [((slots // LANES, LANES), F32)],
        (got,),
    )
    mid, west, east = exchange(low, high)
    lam = jnp.broadcast_to(jnp.concatenate([lst_weights, lst_weights])[:, None], (SUB, LANES))
    inner = (tile_cols // 2 * SUB, LANES)
    image, image_next, seen, seen_next, parts = call(
        functools.partial(solve_kernel, fields),
        [(inner, F32)] * 2 + [((tile_rows, LANES), F32)] * 2 + [((devices, LANES), F32)],
        (north8, east8, scale8, mid, west, east, lam),
        scratch=(
            pltpu.VMEM((span * SUB, LANES), F32),
            pltpu.VMEM((2, tile_cols + 2 * RIM, LANES), F32),
            pltpu.VMEM(inner, F32),
            pltpu.VMEM(inner, F32),
            pltpu.VMEM((2,) + inner, F32),
        ),
        flops=10**9,
        nbytes=10**7,
    )
    parts = lax.all_to_all(parts, AXES, split_axis=0, concat_axis=0, tiled=True)
    back, coef = call(
        answer_kernel,
        [((slots, LANES), F32), ((SUB, LANES), F32)],
        (parts, seen, seen_next, ids),
    )
    back = lax.all_to_all(
        back.reshape(devices, capacity, LANES), AXES, split_axis=0, concat_axis=0, tiled=True
    ).reshape(slots, LANES)
    (increment,) = call(
        functools.partial(increment_kernel, fields),
        [((fields, tile_rows, tile_cols), F32)],
        (image, image_next, coef),
        nbytes=10**6,
    )
    (departure,) = call(depart_kernel, [((tiles, width), F32)], (back, slot, offsets, innovation))
    return increment, departure


def solution(mesh):
    grid = P(None, "lat", "lon")
    tile = P(AXES, None)
    in_specs = (grid, grid, grid, P("lat", "lon"), P(), tile, tile, tile, P(AXES), tile)
    return jax.shard_map(on_device, mesh=mesh, in_specs=in_specs, out_specs=(grid, tile), check_vma=False)
```

```python
import functools

import jax
import jax.numpy as jnp
from jax import lax
from jax.experimental import pallas as pl
from jax.experimental.pallas import tpu as pltpu
from jax.sharding import PartitionSpec as P

PASSES = 8
RIM = 4 * PASSES
LANES = 128
SUB = 8
GROUP = 8
STEP = 4
REACH = LANES // STEP
LOW_BITS = 5
LOW = 2**LOW_BITS
AXES = ("lat", "lon")
F32 = jnp.float32
BF16 = jnp.bfloat16


def iota(shape, dim):
    return lax.broadcasted_iota(jnp.int32, shape, dim)


def call(kernel, outs, args, scratch=(), smem=(), hbm=(), flops=1000, nbytes=100000):
    spaces = [pltpu.VMEM] * len(args)
    for index in smem:
        spaces[index] = pltpu.SMEM
    for index in hbm:
        spaces[index] = pltpu.HBM
    args = [
        pltpu.with_memory_space_constraint(arg, pltpu.HBM) if space == pltpu.HBM else arg
        for arg, space in zip(args, spaces)
    ]
    return pl.pallas_call(
        kernel,
        out_shape=[jax.ShapeDtypeStruct(shape, dtype) for shape, dtype in outs],
        in_specs=[pl.BlockSpec(memory_space=space) for space in spaces],
        out_specs=[pl.BlockSpec(memory_space=pltpu.VMEM)] * len(outs),
        scratch_shapes=list(scratch),
        compiler_params=pltpu.CompilerParams(vmem_limit_bytes=20 * 2**20),
        cost_estimate=pl.CostEstimate(flops=flops, bytes_accessed=nbytes, transcendentals=0),
    )(*args)


def fetch(sources, targets, sems):
    copies = [
        pltpu.make_async_copy(source, target, sems.at[index])
        for index, (source, target) in enumerate(zip(sources, targets))
    ]
    for copy in copies:
        copy.start()
    return copies


def split(value):
    high = value.astype(BF16)
    low = (value - high.astype(F32)).astype(BF16)
    return high, low


def contract(left, right, dims):
    return lax.dot_general(left, right, (dims, ((), ())), preferred_element_type=F32)


def swap_blocks(x, sub, lane):
    block = lane // LOW
    own = sub % 4
    up = pltpu.roll(pltpu.roll(x, SUB - 1, 0), LOW, 1)
    down = pltpu.roll(pltpu.roll(x, 1, 0), LANES - LOW, 1)
    odd_row, odd_block = own % 2, block % 2
    x = jnp.where(odd_row == odd_block, x, jnp.where(odd_row == 0, up, down))
    turned = pltpu.roll(x, 2 * LOW, 1)
    up = pltpu.roll(turned, SUB - 2, 0)
    down = pltpu.roll(turned, 2, 0)
    high_row, high_block = own // 2, block // 2
    return jnp.where(high_row == high_block, x, jnp.where(high_row == 0, up, down))


def route_kernel(devices, capacity, *refs):
    me_ref, sources = refs[0], refs[1:6]
    send_ref, slot_ref, rows_ref, packed_ref = refs[6:10]
    owner_ref, rid_ref, inn_ref, var_ref, off_ref = local = refs[10:15]
    copies = fetch(sources, local, refs[15])
    copies[0].wait()
    copies[1].wait()
    tiles = off_ref.shape[0]
    per_row = LANES // capacity
    hits = (owner_ref[...] == iota((devices, tiles), 0)).astype(F32)
    earlier = (iota((tiles, tiles), 0) < iota((tiles, tiles), 1)).astype(F32).astype(BF16)
    before = jnp.dot(hits.astype(BF16), earlier, preferred_element_type=F32)
    rank = jnp.sum(hits * before, axis=0, keepdims=True)
    slot_row = owner_ref[...] * capacity + rank.astype(jnp.int32)
    slot_ref[...] = jnp.transpose(jnp.broadcast_to(slot_row.astype(F32), (LANES, tiles)))
    shift = (me_ref[0] % per_row) * capacity
    rank_hot = (rank.astype(jnp.int32) + shift == iota((LANES, tiles), 0)).astype(F32).astype(BF16)
    marked = hits * (rid_ref[...].astype(F32) + 1.0)
    ids = contract(marked.astype(BF16), rank_hot, ((1,), (1,)))
    spare = send_ref.shape[1] - 2 * capacity
    pad_row = iota((devices, spare, LANES), 1)
    send_ref[:, 2 * capacity :, :] = jnp.where(
        pad_row == 0, jnp.broadcast_to(ids[:, None, :], (devices, spare, LANES)), 0.0
    )

    for copy in copies[2:]:
        copy.wait()
    sub = iota((SUB, LANES), 0)
    lane = iota((SUB, LANES), 1)
    tall = iota((LOW, LANES), 0)

    def expand(index, carry):
        start = pl.multiple_of(index * GROUP, GROUP)
        window = pl.ds(start, GROUP)
        offsets = off_ref[window, :]
        weight = var_ref[window, :]
        value = weight * inn_ref[window, :]
        low = offsets & (LOW - 1)
        high = offsets >> LOW_BITS
        hot, parts = [], []
        for tile in range(GROUP):
            pick = slice(tile, tile + 1)
            hot.append((low[pick, :] == tall).astype(F32).astype(BF16))
            both = jnp.where(sub < 4, value[pick, :], weight[pick, :])
            parts.append(jnp.where(high[pick, :] == sub % 4, both, 0.0))
        upper, lower = split(jnp.concatenate(parts, 0))
        product = contract(jnp.concatenate([upper, lower], 0), jnp.concatenate(hot, 0), ((1,), (1,)))
        half = GROUP * SUB
        total = product[:half] + product[half:]
        quads = []
        for side in range(2):
            lanes = slice(side * LANES, (side + 1) * LANES)
            merged = total[side * 4 * SUB : (side * 4 + 1) * SUB, lanes]
            for tile in range(1, 4):
                base = (side * 4 + tile) * SUB
                merged = jnp.where(lane // LOW == tile, total[base : base + SUB, lanes], merged)
            quads.append(swap_blocks(merged, sub, lane))
        first, second = quads
        rows_ref[window, 0:LANES] = jnp.where(sub < 4, first, pltpu.roll(second, 4, 0))
        rows_ref[window, LANES : 2 * LANES] = jnp.where(sub < 4, pltpu.roll(first, 4, 0), second)
        return carry

    lax.fori_loop(0, tiles // GROUP, expand, 0, unroll=32)
    upper, lower = split(rows_ref[...])
    slots = devices * capacity
    place = (iota((slots, tiles), 0) == slot_row).astype(F32).astype(BF16)
    packed_ref[...] = jnp.dot(place, upper, preferred_element_type=F32)
    packed_ref[...] += jnp.dot(place, lower, preferred_element_type=F32)
    for side in range(2):
        lanes = slice(side * LANES, (side + 1) * LANES)
        send_ref[:, side * capacity : (side + 1) * capacity, :] = packed_ref[:, lanes].reshape(
            devices, capacity, LANES
        )


def collect_kernel(capacity, got_ref, low_ref, high_ref, ids_ref):
    devices = got_ref.shape[0]
    per_row = LANES // capacity
    rows = 2 * low_ref.shape[1]
    total = jnp.zeros((rows, 2 * LANES), F32)
    line = iota((rows, LANES), 0)
    tall = line // RIM * RIM + STEP * (line % SUB) + line % RIM // SUB + 1
    for block in range(devices // per_row):
        owners = slice(block * per_row, (block + 1) * per_row)
        ids = jnp.sum(got_ref[owners, 2 * capacity : 2 * capacity + SUB, :], axis=0)[0:1, :]
        ids_ref[block : block + 1, :] = ids
        hot = (ids.astype(jnp.int32) == tall).astype(F32).astype(BF16)
        values = jnp.concatenate(
            [
                got_ref[owners, 0:capacity, :].reshape(LANES, LANES),
                got_ref[owners, capacity : 2 * capacity, :].reshape(LANES, LANES),
            ],
            1,
        )
        upper, lower = split(values)
        total = total + contract(
            jnp.concatenate([hot, hot], 1), jnp.concatenate([upper, lower], 0), ((1,), (0,))
        )
    half = rows // 2
    for plane in range(2):
        lanes = slice(plane * LANES, (plane + 1) * LANES)
        low_ref[plane] = total[0:half, lanes]
        high_ref[plane] = total[half:, lanes]


def faces_kernel(fields, last_ref, *refs):
    sources, low_ref, high_ref = refs[0:4], refs[4], refs[5]
    lat_ref, lon_ref, std_ref, mask_ref = local = refs[6:10]
    copies = fetch(sources, local, refs[10])
    for copy in copies:
        copy.wait()
    final = (iota((SUB, LANES), 0) == SUB - 1) & (last_ref[0] == 1)
    for part, target in enumerate((low_ref, high_ref)):
        for step in range(STEP):
            rows = pl.ds(part * RIM + step, SUB, stride=STEP)
            place = slice(step * SUB, (step + 1) * SUB)
            mask = mask_ref[rows, :].astype(F32)
            for field in range(fields):
                face = lat_ref[field, rows, :]
                if part == 1 and step == STEP - 1:
                    face = jnp.where(final, 0.0, face)
                target[field, place, :] = face
                target[fields + field, place, :] = lon_ref[field, rows, :]
                target[2 * fields + field, place, :] = mask * std_ref[field, rows, :]


def turn_kernel(order, low_ref, high_ref, south_ref, north_ref, mid_ref, first_ref, last_ref):
    for plane, pieces in enumerate(order):
        tall = jnp.concatenate(
            [
                ref[source, step * SUB : (step + 1) * SUB, :]
                for source, step in pieces
                for ref in (south_ref, low_ref, high_ref, north_ref)
            ],
            0,
        )
        turned = jnp.transpose(tall)
        mid_ref[plane] = turned
        first_ref[plane] = turned[0:RIM]
        last_ref[plane] = turned[turned.shape[0] - RIM :]


def at(index):
    return slice(index * SUB, (index + 1) * SUB)


def weave_kernel(mid_ref, west_ref, east_ref, north_ref, east_face_ref, scale_ref, wide_ref):
    cols = mid_ref.shape[1]
    length = cols + 2 * RIM
    count = length // SUB
    for plane in range(mid_ref.shape[0]):
        wide_ref[plane, 0:RIM, :] = west_ref[plane]
        wide_ref[plane, RIM : RIM + cols, :] = mid_ref[plane]
        wide_ref[plane, RIM + cols :, :] = east_ref[plane]
    for kind, target in enumerate((north_ref, east_face_ref, scale_ref)):
        for step in range(STEP):
            for j in range(count):
                target[at(j * STEP + step), :] = wide_ref[
                    kind * STEP + step, pl.ds(j, SUB, stride=count), :
                ]


def solve_kernel(
    north_ref,
    east_ref,
    scale_ref,
    mid_ref,
    west_ref,
    far_ref,
    lam_ref,
    image_ref,
    image_next_ref,
    seen_ref,
    seen_next_ref,
    parts_ref,
    u_ref,
    wide_ref,
    grid_ref,
    rhs_ref,
    turn_ref,
    t_ref,
    line_ref,
):
    cols = mid_ref.shape[1]
    length = cols + 2 * RIM
    count = length // SUB
    total = count * STEP
    lam = lam_ref[...]
    sub = iota((SUB, LANES), 0)
    lane = iota((SUB, LANES), 1)
    group = lane // REACH
    inner = (lane % REACH >= RIM // STEP) & (lane % REACH < REACH - RIM // STEP)
    for plane in range(2):
        wide_ref[plane, 0:RIM, :] = west_ref[plane]
        wide_ref[plane, RIM : RIM + cols, :] = mid_ref[plane]
        wide_ref[plane, RIM + cols :, :] = far_ref[plane]
        for j in range(count):
            x = wide_ref[plane, pl.ds(j, SUB, stride=count), :]
            even = jnp.where(group % 2 == 0, x, pltpu.roll(x, REACH, 1))
            odd = jnp.where(group % 2 == 1, x, pltpu.roll(x, LANES - REACH, 1))
            for parity, y in enumerate((even, odd)):
                turned = pltpu.roll(y, 2 * REACH, 1)
                grid_ref[plane, at(j * STEP + parity), :] = jnp.where(group < 2, y, turned)
                grid_ref[plane, at(j * STEP + 2 + parity), :] = jnp.where(group < 2, turned, y)

    def group_sum(x):
        x = x + pltpu.roll(x, 2 * REACH, 1)
        return x + pltpu.roll(x, REACH, 1)

    def diffuse():
        def one_pass(index, carry):
            here = [u_ref[at(step), :] for step in range(STEP)]
            seam = []
            for step in range(STEP):
                final = (count - 1) * STEP + step
                ahead = pltpu.roll(here[step], SUB - 1, 0)
                seam.append(east_ref[at(final), :] * (ahead - u_ref[at(final), :]))
            west = [pltpu.roll(flux, 1, 0) for flux in seam]
            for j in range(count):
                base = j * STEP
                if j + 1 < count:
                    ahead = [u_ref[at(base + STEP + step), :] for step in range(STEP)]
                    flux = [
                        east_ref[at(base + step), :] * (ahead[step] - here[step]) for step in range(STEP)
                    ]
                else:
                    ahead, flux = here, seam
                above = here[1:] + [pltpu.roll(here[0], LANES - 1, 1)]
                rise = [north_ref[at(base + step), :] * (above[step] - here[step]) for step in range(STEP)]
                below = [pltpu.roll(rise[STEP - 1], 1, 1)] + rise[:-1]
                for step in range(STEP):
                    u_ref[at(base + step), :] = here[step] + (
                        (flux[step] - west[step]) + (rise[step] - below[step])
                    )
                west, here = flux, ahead
            return carry

        lax.fori_loop(0, PASSES, one_pass, 0)

    zero = jnp.zeros((SUB, LANES), F32)
    own = [
        inner & (count * sub + j >= RIM) & (count * sub + j < RIM + cols) for j in range(count)
    ]
    spans = {}
    for j in range(count):
        edges = tuple(RIM <= count * row + j < RIM + cols for row in range(SUB))
        spans.setdefault(edges, []).append(j)

    def whole(terms, extra=None):
        out = zero
        for members in spans.values():
            keep = own[members[0]] if extra is None else own[members[0]] & extra
            out = out + jnp.where(keep, sum((terms(j) for j in members), zero), 0.0)
        return jnp.sum(jnp.sum(out, axis=1, keepdims=True), axis=0, keepdims=True)

    def ratio(top, bottom):
        return jnp.where(bottom > 0, top / jnp.where(bottom > 0, bottom, 1.0), 0.0)

    def over_steps(term):
        return lambda j: sum((term(j * STEP + step) for step in range(STEP)), zero)

    for index in range(total):
        u_ref[at(index), :] = lam * scale_ref[at(index), :] * grid_ref[0, at(index), :]
    diffuse()
    for index in range(total):
        rhs_ref[at(index), :] = u_ref[at(index), :]
    diffuse()
    for index in range(total):
        scale = scale_ref[at(index), :]
        image = scale * u_ref[at(index), :]
        seen = group_sum(lam * image)
        image_ref[at(index), :] = image
        t_ref[0, at(index), :] = seen
        u_ref[at(index), :] = lam * scale * (grid_ref[1, at(index), :] * seen)
    diffuse()
    for index in range(total):
        turn_ref[at(index), :] = u_ref[at(index), :]
    diffuse()
    for index in range(total):
        image = scale_ref[at(index), :] * u_ref[at(index), :]
        image_next_ref[at(index), :] = image
        t_ref[1, at(index), :] = group_sum(lam * image)

    once = group == 0
    bb = whole(over_steps(lambda n: rhs_ref[at(n), :] * rhs_ref[at(n), :]))
    bw = whole(over_steps(lambda n: rhs_ref[at(n), :] * turn_ref[at(n), :]))
    weighted = lambda n: grid_ref[1, at(n), :] * t_ref[0, at(n), :]
    s00 = whole(over_steps(lambda n: weighted(n) * t_ref[0, at(n), :]), once)
    s01 = whole(over_steps(lambda n: weighted(n) * t_ref[1, at(n), :]), once)
    fit, seen_fit = ratio(bw, bb), ratio(s01, s00)

    def left(n):
        gap = turn_ref[at(n), :] - fit * rhs_ref[at(n), :]
        return gap * gap

    def seen_left(n):
        gap = t_ref[1, at(n), :] - seen_fit * t_ref[0, at(n), :]
        return grid_ref[1, at(n), :] * (gap * gap)

    rest, seen_rest = whole(over_steps(left)), whole(over_steps(seen_left), once)
    wide = iota(parts_ref.shape, 1)
    parts = jnp.zeros(parts_ref.shape, F32)
    for position, number in enumerate((bb, bw, fit, rest, s00, seen_fit, seen_rest)):
        parts = jnp.where(wide == position, number, parts)
    parts_ref[...] = parts
    edge = RIM // STEP
    for plane, target in enumerate((seen_ref, seen_next_ref)):
        for j in range(count):
            x = t_ref[plane, at(j * STEP), :]
            for step in range(1, STEP):
                x = jnp.where(group == step, t_ref[plane, at(j * STEP + step), :], x)
            line_ref[pl.ds(j, SUB, stride=count), :] = x
        flat = jnp.transpose(line_ref[RIM : RIM + cols, :])
        depth = REACH - 2 * edge
        for step in range(STEP):
            start = step * REACH + edge
            target[step * depth : (step + 1) * depth, :] = flat[start : start + depth]


def pack_kernel(seen_ref, seen_next_ref, ids_ref, both_ref):
    rows = seen_ref.shape[0]
    blocks = ids_ref.shape[0]
    upper, lower = split(jnp.concatenate([seen_ref[...], seen_next_ref[...]], 1))
    both = jnp.concatenate([upper, lower], 0)
    ids = jnp.transpose(jnp.concatenate([ids_ref[...]] * (LANES // blocks), 0)).astype(jnp.int32)
    line = iota((LANES, 2 * rows), 1) % rows
    depth = rows // STEP
    wide = STEP * (line % depth) + line // depth + 1
    hot = jnp.concatenate(
        [(ids[:, block : block + 1] == wide).astype(F32).astype(BF16) for block in range(blocks)], 0
    )
    both_ref[...] = jnp.dot(hot, both, preferred_element_type=F32)


def answer_kernel(parts_ref, both_ref, back_ref, coef_ref):

    def column(index):
        return parts_ref[:, index : index + 1]

    def add(x):
        return jnp.sum(x, axis=0, keepdims=True)

    bb_each, fit_each, s00_each, seen_fit_each = column(0), column(2), column(4), column(5)
    bb, bw = add(bb_each), add(column(1))
    fit = bw / bb
    step = bb / (bb + bw)
    gap = fit_each - fit
    rest = add(column(3) + gap * (gap * bb_each))
    tilt = step * rest / bb
    full = fit + tilt
    gap = seen_fit_each - full
    energy = rest + tilt * tilt * bb + add(column(6) + gap * (gap * s00_each))
    step_next = jnp.where(rest > 0, rest / jnp.where(rest > 0, energy, 1.0), 0.0)
    coef = step * (1.0 + step_next * full)
    coef_next = -step * step_next
    line = iota(coef_ref.shape, 0)
    coef_ref[...] = jnp.where(line == 0, coef, coef_next)
    back_ref[...] = coef * both_ref[:, 0:LANES] + coef_next * both_ref[:, LANES:]


def increment_kernel(image_ref, image_next_ref, coef_ref, out_ref, line_ref):
    fields, _, cols = out_ref.shape
    count = image_ref.shape[0] // (SUB * STEP)
    coef, coef_next = coef_ref[0:1, :], coef_ref[1:2, :]
    edge = RIM // STEP
    depth = REACH - 2 * edge
    for step in range(STEP):
        for j in range(count):
            index = at(j * STEP + step)
            line_ref[step, pl.ds(j, SUB, stride=count), :] = (
                coef * image_ref[index, :] + coef_next * image_next_ref[index, :]
            )
        flat = jnp.transpose(line_ref[step, RIM : RIM + cols, :])
        for field in range(fields):
            start = field * REACH + edge
            out_ref[field, pl.ds(step, depth, stride=STEP), :] = flat[start : start + depth]


def depart_kernel(back_ref, slot_ref, off_ref, inn_ref, out_ref):
    slots = back_ref.shape[0]
    upper, lower = split(back_ref[...])
    slot = slot_ref[...].astype(jnp.int32)
    line = iota((LANES, LANES), 1)
    place = jnp.concatenate(
        [
            jnp.concatenate(
                [
                    (slot[block * LANES : (block + 1) * LANES] == line + part * LANES).astype(F32).astype(BF16)
                    for part in range(slots // LANES)
                ],
                1,
            )
            for block in range(slot.shape[0] // LANES)
        ],
        0,
    )
    rows = jnp.dot(place, jnp.concatenate([upper, lower], 1), preferred_element_type=F32)
    seen = jnp.take_along_axis(rows[:, 0:LANES] + rows[:, LANES:], off_ref[...], axis=1)
    out_ref[...] = inn_ref[...] - seen


def neighbours(low, high, axis, periodic):
    count = lax.axis_size(axis)
    forward = [(i, i + 1) for i in range(count - 1)]
    if periodic:
        forward.append((count - 1, 0))
    backward = [(target, source) for source, target in forward]
    return lax.ppermute(high, axis, forward), lax.ppermute(low, axis, backward)


def exchange(low, high, order):
    planes = len(order)
    south, north = neighbours(low, high, "lat", False)
    mid, first, last = call(
        functools.partial(turn_kernel, order),
        [((planes, LANES, LANES), F32), ((planes, RIM, LANES), F32), ((planes, RIM, LANES), F32)],
        (low, high, south, north),
        nbytes=4 * planes * 300 * LANES,
    )
    west, east = neighbours(first, last, "lon", True)
    return mid, west, east


def analyse(
    lat_coef, lon_coef, std_scale, land_mask, lst_weights, innovation, inv_var, owner, row_ids, offsets
):
    fields, tile_rows, tile_cols = lat_coef.shape
    tiles, width = innovation.shape
    lat_count, lon_count = lax.axis_size("lat"), lax.axis_size("lon")
    devices = lat_count * lon_count
    capacity = max(2, 2 * tiles // devices)
    if (fields * REACH, tile_cols, width, tile_rows + 2 * RIM) != (LANES,) * 4:
        raise ValueError("tile shape")
    if RIM > tile_rows // 2 or capacity % SUB or LANES % capacity or tiles % LANES:
        raise ValueError("slot shape")
    half = tile_rows // 2
    slots = devices * capacity
    last = (lax.axis_index("lat") == lat_count - 1).astype(jnp.int32).reshape(1)
    me = (lax.axis_index("lat") * lon_count + lax.axis_index("lon")).astype(jnp.int32).reshape(1)

    face_low, face_high = call(
        functools.partial(faces_kernel, fields),
        [((3 * fields, half, LANES), F32)] * 2,
        (last, lat_coef, lon_coef, std_scale, land_mask),
        scratch=[pltpu.VMEM(x.shape, x.dtype) for x in (lat_coef, lon_coef, std_scale, land_mask)]
        + [pltpu.SemaphoreType.DMA((4,))],
        smem=(0,),
        hbm=(1, 2, 3, 4),
    )
    face_low, face_high, owner = lax.optimization_barrier((face_low, face_high, owner))
    block = 2 * capacity + SUB
    tables = (owner.reshape(1, tiles), row_ids.reshape(1, tiles), innovation, inv_var, offsets)
    send, slot = call(
        functools.partial(route_kernel, devices, capacity),
        [((devices, block, LANES), F32), ((tiles, LANES), F32)],
        (me,) + tables,
        scratch=[pltpu.VMEM((tiles, 2 * LANES), F32), pltpu.VMEM((slots, 2 * LANES), F32)]
        + [pltpu.VMEM(x.shape, x.dtype) for x in tables]
        + [pltpu.SemaphoreType.DMA((len(tables),))],
        smem=(0,),
        hbm=range(1, 1 + len(tables)),
        flops=10**9,
        nbytes=10**7,
    )
    face_mid, face_west, face_east = exchange(
        face_low,
        face_high,
        [[(kind * fields + field, step) for field in range(fields)] for kind in range(3) for step in range(STEP)],
    )
    got = lax.all_to_all(send, AXES, split_axis=0, concat_axis=0, tiled=True)
    span = tile_cols + 2 * RIM
    woven = (span * STEP, LANES)
    north8, east8, scale8 = call(
        weave_kernel,
        [(woven, F32)] * 3,
        (face_mid, face_west, face_east),
        scratch=(pltpu.VMEM((3 * STEP, span, LANES), F32),),
        nbytes=3 * 10**6,
    )
    low, high, ids = call(
        functools.partial(collect_kernel, capacity),
        [((2, half, LANES), F32)] * 2 + [((slots // LANES, LANES), F32)],
        (got,),
    )
    mid, west, east = exchange(low, high, [[(plane, step) for step in range(STEP)] for plane in range(2)])
    lam = jnp.broadcast_to(jnp.repeat(lst_weights, REACH)[None, :], (SUB, LANES))
    image, image_next, seen, seen_next, parts = call(
        solve_kernel,
        [(woven, F32)] * 2 + [((tile_rows, LANES), F32)] * 2 + [((devices, LANES), F32)],
        (north8, east8, scale8, mid, west, east, lam),
        scratch=(
            pltpu.VMEM(woven, F32),
            pltpu.VMEM((2, span, LANES), F32),
            pltpu.VMEM((2,) + woven, F32),
            pltpu.VMEM(woven, F32),
            pltpu.VMEM(woven, F32),
            pltpu.VMEM((2,) + woven, F32),
            pltpu.VMEM((span, LANES), F32),
        ),
        flops=10**9,
        nbytes=10**7,
    )
    (both,) = call(pack_kernel, [((slots, 2 * LANES), F32)], (seen, seen_next, ids), nbytes=10**6)
    parts = lax.all_to_all(parts, AXES, split_axis=0, concat_axis=0, tiled=True)
    back, coef = call(
        answer_kernel, [((slots, LANES), F32), ((SUB, LANES), F32)], (parts, both), nbytes=10**6
    )
    back = lax.all_to_all(
        back.reshape(devices, capacity, LANES), AXES, split_axis=0, concat_axis=0, tiled=True
    ).reshape(slots, LANES)
    (increment,) = call(
        increment_kernel,
        [((fields, tile_rows, tile_cols), F32)],
        (image, image_next, coef),
        scratch=(pltpu.VMEM((STEP, span, LANES), F32),),
        nbytes=10**6,
    )
    (departure,) = call(depart_kernel, [((tiles, width), F32)], (back, slot, offsets, innovation))
    return increment, departure


def solution(mesh):
    grid = P(None, "lat", "lon")
    tile = P(AXES, None)
    in_specs = (grid, grid, grid, P("lat", "lon"), P(), tile, tile, tile, P(AXES), tile)
    return jax.shard_map(analyse, mesh=mesh, in_specs=in_specs, out_specs=(grid, tile), check_vma=False)
```

```python
import functools

import jax
import jax.numpy as jnp
from jax import lax
from jax.experimental import pallas as pl
from jax.experimental.pallas import tpu as pltpu
from jax.sharding import PartitionSpec as P

PASSES = 8
RIM = 4 * PASSES
LANES = 128
SUB = 8
GROUP = 8
STEP = 4
REACH = LANES // STEP
LOW_BITS = 5
LOW = 2**LOW_BITS
AXES = ("lat", "lon")
F32 = jnp.float32
BF16 = jnp.bfloat16


def iota(shape, dim):
    return lax.broadcasted_iota(jnp.int32, shape, dim)


def call(kernel, outs, args, scratch=(), hbm=(), flops=1000, nbytes=100000):
    spaces = [pltpu.VMEM] * len(args)
    for index in hbm:
        spaces[index] = pltpu.HBM
    args = [
        pltpu.with_memory_space_constraint(arg, pltpu.HBM) if space == pltpu.HBM else arg
        for arg, space in zip(args, spaces)
    ]
    return pl.pallas_call(
        kernel,
        out_shape=[jax.ShapeDtypeStruct(shape, dtype) for shape, dtype in outs],
        in_specs=[pl.BlockSpec(memory_space=space) for space in spaces],
        out_specs=[pl.BlockSpec(memory_space=pltpu.VMEM)] * len(outs),
        scratch_shapes=list(scratch),
        compiler_params=pltpu.CompilerParams(vmem_limit_bytes=20 * 2**20),
        cost_estimate=pl.CostEstimate(flops=flops, bytes_accessed=nbytes, transcendentals=0),
    )(*args)


def fetch(sources, targets, sems):
    copies = [
        pltpu.make_async_copy(source, target, sems.at[index])
        for index, (source, target) in enumerate(zip(sources, targets))
    ]
    for copy in copies:
        copy.start()
    return copies


def split(value):
    high = value.astype(BF16)
    low = (value - high.astype(F32)).astype(BF16)
    return high, low


def contract(left, right, dims):
    return lax.dot_general(left, right, (dims, ((), ())), preferred_element_type=F32)


def swap_blocks(x, sub, lane):
    block = lane // LOW
    own = sub % 4
    up = pltpu.roll(pltpu.roll(x, SUB - 1, 0), LOW, 1)
    down = pltpu.roll(pltpu.roll(x, 1, 0), LANES - LOW, 1)
    odd_row, odd_block = own % 2, block % 2
    x = jnp.where(odd_row == odd_block, x, jnp.where(odd_row == 0, up, down))
    turned = pltpu.roll(x, 2 * LOW, 1)
    up = pltpu.roll(turned, SUB - 2, 0)
    down = pltpu.roll(turned, 2, 0)
    high_row, high_block = own // 2, block // 2
    return jnp.where(high_row == high_block, x, jnp.where(high_row == 0, up, down))


def route_kernel(devices, capacity, *refs):
    flags_ref, sources = refs[0], refs[1:6]
    send_ref, slot_ref, rows_ref, packed_ref = refs[6:10]
    owner_ref, rid_ref, inn_ref, var_ref, off_ref = local = refs[10:15]
    copies = fetch(sources, local, refs[15])
    copies[0].wait()
    copies[1].wait()
    tiles = off_ref.shape[0]
    per_row = LANES // capacity
    hits = (owner_ref[...] == iota((devices, tiles), 0)).astype(F32)
    earlier = (iota((tiles, tiles), 0) < iota((tiles, tiles), 1)).astype(F32).astype(BF16)
    before = jnp.dot(hits.astype(BF16), earlier, preferred_element_type=F32)
    rank = jnp.sum(hits * before, axis=0, keepdims=True)
    slot_row = owner_ref[...] * capacity + rank.astype(jnp.int32)
    slot_ref[...] = jnp.transpose(jnp.broadcast_to(slot_row.astype(F32), (LANES, tiles)))
    shift = (flags_ref[1:2, 0:1] % per_row) * capacity
    rank_hot = (rank.astype(jnp.int32) + shift == iota((LANES, tiles), 0)).astype(F32).astype(BF16)
    marked = hits * (rid_ref[...].astype(F32) + 1.0)
    ids = contract(marked.astype(BF16), rank_hot, ((1,), (1,)))
    block = 2 * capacity + 1
    for device in range(devices):
        place = device * block + 2 * capacity
        send_ref[place : place + 1, :] = ids[device : device + 1, :]
    for copy in copies[2:]:
        copy.wait()
    sub = iota((SUB, LANES), 0)
    lane = iota((SUB, LANES), 1)
    tall = iota((LOW, LANES), 0)

    def expand(index, carry):
        start = pl.multiple_of(index * GROUP, GROUP)
        window = pl.ds(start, GROUP)
        offsets = off_ref[window, :]
        weight = var_ref[window, :]
        value = weight * inn_ref[window, :]
        low = offsets & (LOW - 1)
        high = offsets >> LOW_BITS
        hot, parts = [], []
        for tile in range(GROUP):
            pick = slice(tile, tile + 1)
            hot.append((low[pick, :] == tall).astype(F32).astype(BF16))
            both = jnp.where(sub < 4, value[pick, :], weight[pick, :])
            parts.append(jnp.where(high[pick, :] == sub % 4, both, 0.0))
        upper, lower = split(jnp.concatenate(parts, 0))
        product = contract(jnp.concatenate([upper, lower], 0), jnp.concatenate(hot, 0), ((1,), (1,)))
        half = GROUP * SUB
        total = product[:half] + product[half:]
        quads = []
        for side in range(2):
            lanes = slice(side * LANES, (side + 1) * LANES)
            merged = total[side * 4 * SUB : (side * 4 + 1) * SUB, lanes]
            for tile in range(1, 4):
                base = (side * 4 + tile) * SUB
                merged = jnp.where(lane // LOW == tile, total[base : base + SUB, lanes], merged)
            quads.append(swap_blocks(merged, sub, lane))
        first, second = quads
        rows_ref[window, 0:LANES] = jnp.where(sub < 4, first, pltpu.roll(second, 4, 0))
        rows_ref[window, LANES : 2 * LANES] = jnp.where(sub < 4, pltpu.roll(first, 4, 0), second)
        return carry

    lax.fori_loop(0, tiles // GROUP, expand, 0, unroll=32)
    upper, lower = split(rows_ref[...])
    slots = devices * capacity
    place = (iota((slots, tiles), 0) == slot_row).astype(F32).astype(BF16)
    packed_ref[...] = jnp.dot(place, upper, preferred_element_type=F32)
    packed_ref[...] += jnp.dot(place, lower, preferred_element_type=F32)
    for device in range(devices):
        for side in range(2):
            start = device * block + side * capacity
            send_ref[start : start + capacity, :] = packed_ref[
                device * capacity : (device + 1) * capacity, side * LANES : (side + 1) * LANES
            ]


def by_parity(odd, low, high):
    return jnp.where(odd, low, high), jnp.where(odd, high, low)


def collect_kernel(devices, capacity, flags_ref, got_ref, low_ref, high_ref, ids_ref, first_ref, second_ref):
    block = 2 * capacity + 1
    per_row = LANES // capacity
    rows = 2 * low_ref.shape[1]
    total = jnp.zeros((rows, 2 * LANES), F32)
    line = iota((rows, LANES), 0)
    tall = line // RIM * RIM + STEP * (line % SUB) + line % RIM // SUB + 1

    def piece(device, start, size):
        return got_ref[device * block + start : device * block + start + size, :]

    for group in range(devices // per_row):
        members = range(group * per_row, (group + 1) * per_row)
        ids = sum(piece(device, 2 * capacity, 1) for device in members)
        ids_ref[group : group + 1, :] = ids
        hot = (ids.astype(jnp.int32) == tall).astype(F32).astype(BF16)
        values = jnp.concatenate(
            [
                jnp.concatenate([piece(device, side * capacity, capacity) for device in members], 0)
                for side in range(2)
            ],
            1,
        )
        upper, lower = split(values)
        total = total + contract(
            jnp.concatenate([hot, hot], 1), jnp.concatenate([upper, lower], 0), ((1,), (0,))
        )
    half = rows // 2
    odd = flags_ref[2:3, :] == 1
    for plane in range(2):
        lanes = slice(plane * LANES, (plane + 1) * LANES)
        low, high = total[0:half, lanes], total[half:, lanes]
        low_ref[plane] = low
        high_ref[plane] = high
        first_ref[plane], second_ref[plane] = by_parity(odd, low, high)


def faces_kernel(fields, flags_ref, *refs):
    sources, low_ref, high_ref, first_ref, second_ref = refs[0:4], *refs[4:8]
    lat_ref, lon_ref, std_ref, mask_ref = local = refs[8:12]
    copies = fetch(sources, local, refs[12])
    for copy in copies:
        copy.wait()
    final = (iota((SUB, LANES), 0) == SUB - 1) & (flags_ref[0:1, :] == 1)
    for part, target in enumerate((low_ref, high_ref)):
        for step in range(STEP):
            rows = pl.ds(part * RIM + step, SUB, stride=STEP)
            place = slice(step * SUB, (step + 1) * SUB)
            mask = mask_ref[rows, :].astype(F32)
            for field in range(fields):
                face = lat_ref[field, rows, :]
                if part == 1 and step == STEP - 1:
                    face = jnp.where(final, 0.0, face)
                target[field, place, :] = face
                target[fields + field, place, :] = lon_ref[field, rows, :]
                target[2 * fields + field, place, :] = mask * std_ref[field, rows, :]
    odd = flags_ref[2:3, :] == 1
    for plane in range(3 * fields):
        first_ref[plane], second_ref[plane] = by_parity(odd, low_ref[plane], high_ref[plane])


def turn_kernel(order, flags_ref, low_ref, high_ref, got_ref, other_ref, mid_ref, first_ref, second_ref):
    odd = flags_ref[2:3, :] == 1
    odd_lon = flags_ref[3:4, :] == 1
    for plane, pieces in enumerate(order):
        rows = []
        for source, step in pieces:
            place = slice(step * SUB, (step + 1) * SUB)
            south, north = by_parity(odd, got_ref[source, place, :], other_ref[source, place, :])
            rows.extend([south, low_ref[source, place, :], high_ref[source, place, :], north])
        turned = jnp.transpose(jnp.concatenate(rows, 0))
        mid_ref[plane] = turned
        first_ref[plane], second_ref[plane] = by_parity(
            odd_lon, turned[0:RIM], turned[turned.shape[0] - RIM :]
        )


def at(index):
    return slice(index * SUB, (index + 1) * SUB)


def weave_kernel(flags_ref, mid_ref, got_ref, other_ref, north_ref, east_face_ref, scale_ref, wide_ref):
    cols = mid_ref.shape[1]
    length = cols + 2 * RIM
    count = length // SUB
    for plane in range(mid_ref.shape[0]):
        west, east = by_parity(flags_ref[3:4, :] == 1, got_ref[plane], other_ref[plane])
        wide_ref[plane, 0:RIM, :] = west
        wide_ref[plane, RIM : RIM + cols, :] = mid_ref[plane]
        wide_ref[plane, RIM + cols :, :] = east
    for kind, target in enumerate((north_ref, east_face_ref, scale_ref)):
        for step in range(STEP):
            for j in range(count):
                target[at(j * STEP + step), :] = wide_ref[
                    kind * STEP + step, pl.ds(j, SUB, stride=count), :
                ]


def solve_kernel(
    flags_ref,
    north_ref,
    east_ref,
    scale_ref,
    mid_ref,
    got_ref,
    other_ref,
    lam_ref,
    image_ref,
    image_next_ref,
    seen_ref,
    seen_next_ref,
    parts_ref,
    u_ref,
    wide_ref,
    grid_ref,
    rhs_ref,
    turn_ref,
    t_ref,
    line_ref,
):
    cols = mid_ref.shape[1]
    length = cols + 2 * RIM
    count = length // SUB
    total = count * STEP
    lam = lam_ref[...]
    sub = iota((SUB, LANES), 0)
    lane = iota((SUB, LANES), 1)
    group = lane // REACH
    inner = (lane % REACH >= RIM // STEP) & (lane % REACH < REACH - RIM // STEP)
    for plane in range(2):
        west, east = by_parity(flags_ref[3:4, :] == 1, got_ref[plane], other_ref[plane])
        wide_ref[plane, 0:RIM, :] = west
        wide_ref[plane, RIM : RIM + cols, :] = mid_ref[plane]
        wide_ref[plane, RIM + cols :, :] = east
        for j in range(count):
            x = wide_ref[plane, pl.ds(j, SUB, stride=count), :]
            even = jnp.where(group % 2 == 0, x, pltpu.roll(x, REACH, 1))
            odd = jnp.where(group % 2 == 1, x, pltpu.roll(x, LANES - REACH, 1))
            for parity, y in enumerate((even, odd)):
                turned = pltpu.roll(y, 2 * REACH, 1)
                grid_ref[plane, at(j * STEP + parity), :] = jnp.where(group < 2, y, turned)
                grid_ref[plane, at(j * STEP + 2 + parity), :] = jnp.where(group < 2, turned, y)

    def group_sum(x):
        x = x + pltpu.roll(x, 2 * REACH, 1)
        return x + pltpu.roll(x, REACH, 1)

    def diffuse():
        def one_pass(index, carry):
            here = [u_ref[at(step), :] for step in range(STEP)]
            seam = []
            for step in range(STEP):
                final = (count - 1) * STEP + step
                ahead = pltpu.roll(here[step], SUB - 1, 0)
                seam.append(east_ref[at(final), :] * (ahead - u_ref[at(final), :]))
            west = [pltpu.roll(flux, 1, 0) for flux in seam]
            for j in range(count):
                base = j * STEP
                if j + 1 < count:
                    ahead = [u_ref[at(base + STEP + step), :] for step in range(STEP)]
                    flux = [
                        east_ref[at(base + step), :] * (ahead[step] - here[step]) for step in range(STEP)
                    ]
                else:
                    ahead, flux = here, seam
                above = here[1:] + [pltpu.roll(here[0], LANES - 1, 1)]
                rise = [north_ref[at(base + step), :] * (above[step] - here[step]) for step in range(STEP)]
                below = [pltpu.roll(rise[STEP - 1], 1, 1)] + rise[:-1]
                for step in range(STEP):
                    u_ref[at(base + step), :] = here[step] + (
                        (flux[step] - west[step]) + (rise[step] - below[step])
                    )
                west, here = flux, ahead
            return carry

        lax.fori_loop(0, PASSES, one_pass, 0)

    zero = jnp.zeros((SUB, LANES), F32)
    own = [
        inner & (count * sub + j >= RIM) & (count * sub + j < RIM + cols) for j in range(count)
    ]
    spans = {}
    for j in range(count):
        edges = tuple(RIM <= count * row + j < RIM + cols for row in range(SUB))
        spans.setdefault(edges, []).append(j)

    kind_of = {j: edges for edges, members in spans.items() for j in members}

    def tally():
        return {edges: zero for edges in spans}

    def whole(sums, extra=None):
        out = zero
        for edges, members in spans.items():
            keep = own[members[0]] if extra is None else own[members[0]] & extra
            out = out + jnp.where(keep, sums[edges], 0.0)
        return jnp.sum(jnp.sum(out, axis=1, keepdims=True), axis=0, keepdims=True)

    def ratio(top, bottom):
        return jnp.where(bottom > 0, top / jnp.where(bottom > 0, bottom, 1.0), 0.0)

    once = group == 0
    sum_bb, sum_bw, sum_00, sum_01 = tally(), tally(), tally(), tally()
    for index in range(total):
        u_ref[at(index), :] = lam * scale_ref[at(index), :] * grid_ref[0, at(index), :]
    diffuse()
    for index in range(total):
        rhs = u_ref[at(index), :]
        rhs_ref[at(index), :] = rhs
        sum_bb[kind_of[index // STEP]] += rhs * rhs
    diffuse()
    for index in range(total):
        scale = scale_ref[at(index), :]
        image = scale * u_ref[at(index), :]
        seen = group_sum(lam * image)
        weighted = grid_ref[1, at(index), :] * seen
        image_ref[at(index), :] = image
        t_ref[0, at(index), :] = seen
        u_ref[at(index), :] = lam * scale * weighted
        sum_00[kind_of[index // STEP]] += weighted * seen
    diffuse()
    for index in range(total):
        turn = u_ref[at(index), :]
        turn_ref[at(index), :] = turn
        sum_bw[kind_of[index // STEP]] += turn * rhs_ref[at(index), :]
    diffuse()
    for index in range(total):
        image = scale_ref[at(index), :] * u_ref[at(index), :]
        image_next_ref[at(index), :] = image
        seen = group_sum(lam * image)
        t_ref[1, at(index), :] = seen
        sum_01[kind_of[index // STEP]] += grid_ref[1, at(index), :] * t_ref[0, at(index), :] * seen
    bb, bw, s00, s01 = whole(sum_bb), whole(sum_bw), whole(sum_00, once), whole(sum_01, once)
    fit, seen_fit = ratio(bw, bb), ratio(s01, s00)
    left, seen_left = tally(), tally()
    for index in range(total):
        kind = kind_of[index // STEP]
        gap = turn_ref[at(index), :] - fit * rhs_ref[at(index), :]
        left[kind] += gap * gap
        gap = t_ref[1, at(index), :] - seen_fit * t_ref[0, at(index), :]
        seen_left[kind] += grid_ref[1, at(index), :] * (gap * gap)
    rest, seen_rest = whole(left), whole(seen_left, once)
    wide = iota(parts_ref.shape, 1)
    parts = jnp.zeros(parts_ref.shape, F32)
    for position, number in enumerate((bb, s00, bw, s01, fit, seen_fit, rest, seen_rest)):
        parts = jnp.where(wide == position, number, parts)
    parts_ref[...] = parts
    edge = RIM // STEP
    for plane, target in enumerate((seen_ref, seen_next_ref)):
        for j in range(count):
            x = t_ref[plane, at(j * STEP), :]
            for step in range(1, STEP):
                x = jnp.where(group == step, t_ref[plane, at(j * STEP + step), :], x)
            line_ref[pl.ds(j, SUB, stride=count), :] = x
        flat = jnp.transpose(line_ref[RIM : RIM + cols, :])
        depth = REACH - 2 * edge
        for step in range(STEP):
            start = step * REACH + edge
            target[step * depth : (step + 1) * depth, :] = flat[start : start + depth]


def pack_kernel(seen_ref, seen_next_ref, ids_ref, both_ref):
    rows = seen_ref.shape[0]
    blocks = ids_ref.shape[0]
    upper, lower = split(jnp.concatenate([seen_ref[...], seen_next_ref[...]], 1))
    both = jnp.concatenate([upper, lower], 0)
    ids = jnp.transpose(jnp.concatenate([ids_ref[...]] * (LANES // blocks), 0)).astype(jnp.int32)
    line = iota((LANES, 2 * rows), 1) % rows
    depth = rows // STEP
    wide = STEP * (line % depth) + line // depth + 1
    hot = jnp.concatenate(
        [(ids[:, block : block + 1] == wide).astype(F32).astype(BF16) for block in range(blocks)], 0
    )
    both_ref[...] = jnp.dot(hot, both, preferred_element_type=F32)


def answer_kernel(parts_ref, both_ref, back_ref, coef_ref):
    parts = parts_ref[...]

    def ahead(x, count):
        return pltpu.roll(x, LANES - count, 1)

    def add(x):
        return jnp.broadcast_to(jnp.sum(x, axis=0, keepdims=True), (SUB, LANES))

    sums = add(parts)
    fits = jnp.where(sums > 0, ahead(sums, 2) / sums, 0.0)
    gap = ahead(parts, 4) - fits[0:1, :]
    rests = add(ahead(parts, 6) + gap * (gap * parts))

    def pick(x, lane):
        return x[0:1, lane : lane + 1]

    bb, s00, bw = pick(sums, 0), pick(sums, 1), pick(sums, 2)
    fit, seen_fit = pick(fits, 0), pick(fits, 1)
    rest, seen_rest = pick(rests, 0), pick(rests, 1)
    step = bb / (bb + bw)
    tilt = rest / (bb + bw)
    full = fit + tilt
    gap = seen_fit - full
    energy = rest + tilt * tilt * bb + seen_rest + gap * (gap * s00)
    step_next = jnp.where(rest > 0, rest / jnp.where(rest > 0, energy, 1.0), 0.0)
    coef = step * (1.0 + step_next * full)
    coef_next = -step * step_next
    line = iota(coef_ref.shape, 0)
    coef_ref[...] = jnp.where(line == 0, coef, coef_next)
    back_ref[...] = coef * both_ref[:, 0:LANES] + coef_next * both_ref[:, LANES:]


def increment_kernel(image_ref, image_next_ref, coef_ref, out_ref, line_ref):
    fields, _, cols = out_ref.shape
    count = image_ref.shape[0] // (SUB * STEP)
    coef, coef_next = coef_ref[0:1, :], coef_ref[1:2, :]
    edge = RIM // STEP
    depth = REACH - 2 * edge
    for step in range(STEP):
        for j in range(count):
            index = at(j * STEP + step)
            line_ref[step, pl.ds(j, SUB, stride=count), :] = (
                coef * image_ref[index, :] + coef_next * image_next_ref[index, :]
            )
        flat = jnp.transpose(line_ref[step, RIM : RIM + cols, :])
        for field in range(fields):
            start = field * REACH + edge
            out_ref[field, pl.ds(step, depth, stride=STEP), :] = flat[start : start + depth]


def depart_kernel(back_ref, slot_ref, off_ref, inn_ref, out_ref):
    slots = back_ref.shape[0]
    upper, lower = split(back_ref[...])
    slot = slot_ref[...].astype(jnp.int32)
    line = iota((LANES, LANES), 1)
    place = jnp.concatenate(
        [
            jnp.concatenate(
                [
                    (slot[block * LANES : (block + 1) * LANES] == line + part * LANES).astype(F32).astype(BF16)
                    for part in range(slots // LANES)
                ],
                1,
            )
            for block in range(slot.shape[0] // LANES)
        ],
        0,
    )
    rows = jnp.dot(place, jnp.concatenate([upper, lower], 1), preferred_element_type=F32)
    seen = jnp.take_along_axis(rows[:, 0:LANES] + rows[:, LANES:], off_ref[...], axis=1)
    out_ref[...] = inn_ref[...] - seen


def swap(first, second, axis, periodic):
    count = lax.axis_size(axis)
    pairs = [[(i, i + 1) for i in range(start, count - 1, 2)] for start in (0, 1)]
    if periodic:
        pairs[1].append((count - 1, 0))
    both = [edges + [(target, source) for source, target in edges] for edges in pairs]
    return lax.ppermute(first, axis, both[0]), lax.ppermute(second, axis, both[1])


def exchange(flags, low, high, first, second, order):
    planes = len(order)
    got, other = swap(first, second, "lat", False)
    mid, first, second = call(
        functools.partial(turn_kernel, order),
        [((planes, LANES, LANES), F32), ((planes, RIM, LANES), F32), ((planes, RIM, LANES), F32)],
        (flags, low, high, got, other),
        nbytes=4 * planes * 300 * LANES,
    )
    got, other = swap(first, second, "lon", True)
    return mid, got, other


def analyse(
    lat_coef, lon_coef, std_scale, land_mask, lst_weights, innovation, inv_var, owner, row_ids, offsets
):
    fields, tile_rows, tile_cols = lat_coef.shape
    tiles, width = innovation.shape
    lat_count, lon_count = lax.axis_size("lat"), lax.axis_size("lon")
    devices = lat_count * lon_count
    capacity = max(2, 2 * tiles // devices)
    if (fields * REACH, tile_cols, width, tile_rows + 2 * RIM) != (LANES,) * 4:
        raise ValueError("tile shape")
    if RIM > tile_rows // 2 or lat_count % 2 or lon_count % 2 or capacity % SUB or LANES % capacity or tiles % LANES:
        raise ValueError("slot shape")
    half = tile_rows // 2
    slots = devices * capacity
    lat_index, lon_index = lax.axis_index("lat"), lax.axis_index("lon")
    last = (lat_index == lat_count - 1).astype(jnp.int32)
    flags = jnp.zeros((SUB, LANES), jnp.int32)
    for line, flag in enumerate((last, lat_index * lon_count + lon_index, lat_index % 2, lon_index % 2)):
        flags = jnp.where(iota(flags.shape, 0) == line, flag.astype(jnp.int32), flags)

    face_low, face_high, *face_ends = call(
        functools.partial(faces_kernel, fields),
        [((3 * fields, half, LANES), F32)] * 4,
        (flags, lat_coef, lon_coef, std_scale, land_mask),
        scratch=[pltpu.VMEM(x.shape, x.dtype) for x in (lat_coef, lon_coef, std_scale, land_mask)]
        + [pltpu.SemaphoreType.DMA((4,))],
        hbm=(1, 2, 3, 4),
    )
    block = 2 * capacity + 1
    tables = (owner.reshape(1, tiles), row_ids.reshape(1, tiles), innovation, inv_var, offsets)
    send, slot = call(
        functools.partial(route_kernel, devices, capacity),
        [((devices * block, LANES), F32), ((tiles, LANES), F32)],
        (flags,) + tables,
        scratch=[pltpu.VMEM((tiles, 2 * LANES), F32), pltpu.VMEM((slots, 2 * LANES), F32)]
        + [pltpu.VMEM(x.shape, x.dtype) for x in tables]
        + [pltpu.SemaphoreType.DMA((len(tables),))],
            hbm=range(1, 1 + len(tables)),
        flops=10**9,
        nbytes=10**7,
    )
    face_all = exchange(
        flags,
        face_low,
        face_high,
        *face_ends,
        [[(kind * fields + field, step) for field in range(fields)] for kind in range(3) for step in range(STEP)],
    )
    got = lax.all_to_all(
        send.reshape(devices, 1, block * LANES), AXES, split_axis=0, concat_axis=0, tiled=True
    ).reshape(devices * block, LANES)
    span = tile_cols + 2 * RIM
    woven = (span * STEP, LANES)
    north8, east8, scale8 = call(
        weave_kernel,
        [(woven, F32)] * 3,
        (flags, *face_all),
        scratch=(pltpu.VMEM((3 * STEP, span, LANES), F32),),
        nbytes=3 * 10**6,
    )
    low, high, ids, *ends = call(
        functools.partial(collect_kernel, devices, capacity),
        [((2, half, LANES), F32)] * 2 + [((slots // LANES, LANES), F32)] + [((2, half, LANES), F32)] * 2,
        (flags, got),
    )
    grid = exchange(flags, low, high, *ends, [[(plane, step) for step in range(STEP)] for plane in range(2)])
    lam = jnp.broadcast_to(jnp.repeat(lst_weights, REACH)[None, :], (SUB, LANES))
    image, image_next, seen, seen_next, parts = call(
        solve_kernel,
        [(woven, F32)] * 2 + [((tile_rows, LANES), F32)] * 2 + [((devices, LANES), F32)],
        (flags, north8, east8, scale8, *grid, lam),
        scratch=(
            pltpu.VMEM(woven, F32),
            pltpu.VMEM((2, span, LANES), F32),
            pltpu.VMEM((2,) + woven, F32),
            pltpu.VMEM(woven, F32),
            pltpu.VMEM(woven, F32),
            pltpu.VMEM((2,) + woven, F32),
            pltpu.VMEM((span, LANES), F32),
        ),
        flops=10**9,
        nbytes=10**7,
    )
    (both,) = call(pack_kernel, [((slots, 2 * LANES), F32)], (seen, seen_next, ids), nbytes=10**6)
    parts = lax.all_to_all(parts, AXES, split_axis=0, concat_axis=0, tiled=True)
    back, coef = call(
        answer_kernel, [((slots, LANES), F32), ((SUB, LANES), F32)], (parts, both), nbytes=10**6
    )
    back = lax.all_to_all(
        back.reshape(devices, capacity, LANES), AXES, split_axis=0, concat_axis=0, tiled=True
    ).reshape(slots, LANES)
    (increment,) = call(
        increment_kernel,
        [((fields, tile_rows, tile_cols), F32)],
        (image, image_next, coef),
        scratch=(pltpu.VMEM((STEP, span, LANES), F32),),
        nbytes=10**6,
    )
    (departure,) = call(depart_kernel, [((tiles, width), F32)], (back, slot, offsets, innovation))
    return increment, departure


def solution(mesh):
    grid = P(None, "lat", "lon")
    tile = P(AXES, None)
    in_specs = (grid, grid, grid, P("lat", "lon"), P(), tile, tile, tile, P(AXES), tile)
    return jax.shard_map(analyse, mesh=mesh, in_specs=in_specs, out_specs=(grid, tile), check_vma=False)
```

```python
import functools

import jax
import jax.numpy as jnp
from jax import lax
from jax.experimental import pallas as pl
from jax.experimental.pallas import tpu as pltpu
from jax.sharding import PartitionSpec as P

PASSES = 8
RIM = 4 * PASSES
LANES = 128
SUB = 8
GROUP = 8
STEP = 4
REACH = LANES // STEP
LOW_BITS = 5
LOW = 2**LOW_BITS
AXES = ("lat", "lon")
F32 = jnp.float32
BF16 = jnp.bfloat16


def iota(shape, dim):
    return lax.broadcasted_iota(jnp.int32, shape, dim)


def call(kernel, outs, args, scratch=(), hbm=(), flops=1000, nbytes=100000):
    spaces = [pltpu.VMEM] * len(args)
    for index in hbm:
        spaces[index] = pltpu.HBM
    args = [
        pltpu.with_memory_space_constraint(arg, pltpu.HBM) if space == pltpu.HBM else arg
        for arg, space in zip(args, spaces)
    ]
    return pl.pallas_call(
        kernel,
        out_shape=[jax.ShapeDtypeStruct(shape, dtype) for shape, dtype in outs],
        in_specs=[pl.BlockSpec(memory_space=space) for space in spaces],
        out_specs=[pl.BlockSpec(memory_space=pltpu.VMEM)] * len(outs),
        scratch_shapes=list(scratch),
        compiler_params=pltpu.CompilerParams(vmem_limit_bytes=20 * 2**20),
        cost_estimate=pl.CostEstimate(flops=flops, bytes_accessed=nbytes, transcendentals=0),
    )(*args)


def fetch(sources, targets, sems):
    copies = [
        pltpu.make_async_copy(source, target, sems.at[index])
        for index, (source, target) in enumerate(zip(sources, targets))
    ]
    for copy in copies:
        copy.start()
    return copies


def split(value):
    high = value.astype(BF16)
    low = (value - high.astype(F32)).astype(BF16)
    return high, low


def contract(left, right, dims):
    return lax.dot_general(left, right, (dims, ((), ())), preferred_element_type=F32)


def swap_blocks(x, sub, lane):
    block = lane // LOW
    own = sub % 4
    up = pltpu.roll(pltpu.roll(x, SUB - 1, 0), LOW, 1)
    down = pltpu.roll(pltpu.roll(x, 1, 0), LANES - LOW, 1)
    odd_row, odd_block = own % 2, block % 2
    x = jnp.where(odd_row == odd_block, x, jnp.where(odd_row == 0, up, down))
    turned = pltpu.roll(x, 2 * LOW, 1)
    up = pltpu.roll(turned, SUB - 2, 0)
    down = pltpu.roll(turned, 2, 0)
    high_row, high_block = own // 2, block // 2
    return jnp.where(high_row == high_block, x, jnp.where(high_row == 0, up, down))


def route_kernel(devices, capacity, *refs):
    flags_ref, sources = refs[0], refs[1:6]
    send_ref, slot_ref, rows_ref, packed_ref = refs[6:10]
    owner_ref, rid_ref, inn_ref, var_ref, off_ref = sources
    tiles = off_ref.shape[0]
    per_row = LANES // capacity
    hits = (owner_ref[...] == iota((devices, tiles), 0)).astype(F32)
    earlier = (iota((tiles, tiles), 0) < iota((tiles, tiles), 1)).astype(F32).astype(BF16)
    before = jnp.dot(hits.astype(BF16), earlier, preferred_element_type=F32)
    rank = jnp.sum(hits * before, axis=0, keepdims=True)
    slot_row = owner_ref[...] * capacity + rank.astype(jnp.int32)
    slot_ref[...] = jnp.transpose(jnp.broadcast_to(slot_row.astype(F32), (LANES, tiles)))
    shift = (flags_ref[1:2, 0:1] % per_row) * capacity
    rank_hot = (rank.astype(jnp.int32) + shift == iota((LANES, tiles), 0)).astype(F32).astype(BF16)
    marked = hits * (rid_ref[...].astype(F32) + 1.0)
    ids = contract(marked.astype(BF16), rank_hot, ((1,), (1,)))
    block = 2 * capacity + 1
    for device in range(devices):
        place = device * block + 2 * capacity
        send_ref[place : place + 1, :] = ids[device : device + 1, :]
    sub = iota((SUB, LANES), 0)
    lane = iota((SUB, LANES), 1)
    tall = iota((LOW, LANES), 0)

    def expand(index, carry):
        start = pl.multiple_of(index * GROUP, GROUP)
        window = pl.ds(start, GROUP)
        offsets = off_ref[window, :]
        weight = var_ref[window, :]
        value = weight * inn_ref[window, :]
        low = offsets & (LOW - 1)
        high = offsets >> LOW_BITS
        hot, parts = [], []
        for tile in range(GROUP):
            pick = slice(tile, tile + 1)
            hot.append((low[pick, :] == tall).astype(F32).astype(BF16))
            both = jnp.where(sub < 4, value[pick, :], weight[pick, :])
            parts.append(jnp.where(high[pick, :] == sub % 4, both, 0.0))
        upper, lower = split(jnp.concatenate(parts, 0))
        product = contract(jnp.concatenate([upper, lower], 0), jnp.concatenate(hot, 0), ((1,), (1,)))
        half = GROUP * SUB
        total = product[:half] + product[half:]
        quads = []
        for side in range(2):
            lanes = slice(side * LANES, (side + 1) * LANES)
            merged = total[side * 4 * SUB : (side * 4 + 1) * SUB, lanes]
            for tile in range(1, 4):
                base = (side * 4 + tile) * SUB
                merged = jnp.where(lane // LOW == tile, total[base : base + SUB, lanes], merged)
            quads.append(swap_blocks(merged, sub, lane))
        first, second = quads
        rows_ref[window, 0:LANES] = jnp.where(sub < 4, first, pltpu.roll(second, 4, 0))
        rows_ref[window, LANES : 2 * LANES] = jnp.where(sub < 4, pltpu.roll(first, 4, 0), second)
        return carry

    lax.fori_loop(0, tiles // GROUP, expand, 0, unroll=32)
    upper, lower = split(rows_ref[...])
    slots = devices * capacity
    place = (iota((slots, tiles), 0) == slot_row).astype(F32).astype(BF16)
    packed_ref[...] = jnp.dot(place, upper, preferred_element_type=F32)
    packed_ref[...] += jnp.dot(place, lower, preferred_element_type=F32)
    for device in range(devices):
        for side in range(2):
            start = device * block + side * capacity
            send_ref[start : start + capacity, :] = packed_ref[
                device * capacity : (device + 1) * capacity, side * LANES : (side + 1) * LANES
            ]


def by_parity(odd, low, high):
    return jnp.where(odd, low, high), jnp.where(odd, high, low)


def collect_kernel(devices, capacity, flags_ref, got_ref, low_ref, high_ref, ids_ref, first_ref, second_ref):
    block = 2 * capacity + 1
    per_row = LANES // capacity
    rows = 2 * low_ref.shape[1]
    total = jnp.zeros((rows, 2 * LANES), F32)
    line = iota((rows, LANES), 0)
    tall = line // RIM * RIM + STEP * (line % SUB) + line % RIM // SUB + 1

    def piece(device, start, size):
        return got_ref[device * block + start : device * block + start + size, :]

    for group in range(devices // per_row):
        members = range(group * per_row, (group + 1) * per_row)
        ids = sum(piece(device, 2 * capacity, 1) for device in members)
        ids_ref[group : group + 1, :] = ids
        hot = (ids.astype(jnp.int32) == tall).astype(F32).astype(BF16)
        values = jnp.concatenate(
            [
                jnp.concatenate([piece(device, side * capacity, capacity) for device in members], 0)
                for side in range(2)
            ],
            1,
        )
        upper, lower = split(values)
        total = total + contract(
            jnp.concatenate([hot, hot], 1), jnp.concatenate([upper, lower], 0), ((1,), (0,))
        )
    half = rows // 2
    odd = flags_ref[2:3, :] == 1
    for plane in range(2):
        lanes = slice(plane * LANES, (plane + 1) * LANES)
        low, high = total[0:half, lanes], total[half:, lanes]
        low_ref[plane] = low
        high_ref[plane] = high
        first_ref[plane], second_ref[plane] = by_parity(odd, low, high)


def faces_kernel(fields, flags_ref, *refs):
    low_ref, high_ref, first_ref, second_ref = refs[9:13]
    lat_ref, lon_ref, std_ref, mask_ref = local = refs[18:22]
    copies = fetch(refs[0:9], local + refs[13:18], refs[22])
    for copy in copies[0:4]:
        copy.wait()
    final = (iota((SUB, LANES), 0) == SUB - 1) & (flags_ref[0:1, :] == 1)
    for part, target in enumerate((low_ref, high_ref)):
        for step in range(STEP):
            rows = pl.ds(part * RIM + step, SUB, stride=STEP)
            place = slice(step * SUB, (step + 1) * SUB)
            mask = mask_ref[rows, :].astype(F32)
            for field in range(fields):
                face = lat_ref[field, rows, :]
                if part == 1 and step == STEP - 1:
                    face = jnp.where(final, 0.0, face)
                target[field, place, :] = face
                target[fields + field, place, :] = lon_ref[field, rows, :]
                target[2 * fields + field, place, :] = mask * std_ref[field, rows, :]
    odd = flags_ref[2:3, :] == 1
    for plane in range(3 * fields):
        first_ref[plane], second_ref[plane] = by_parity(odd, low_ref[plane], high_ref[plane])
    for copy in copies[4:]:
        copy.wait()


def turn_kernel(order, flags_ref, low_ref, high_ref, got_ref, other_ref, mid_ref, first_ref, second_ref):
    odd = flags_ref[2:3, :] == 1
    odd_lon = flags_ref[3:4, :] == 1
    for plane, pieces in enumerate(order):
        rows = []
        for source, step in pieces:
            place = slice(step * SUB, (step + 1) * SUB)
            south, north = by_parity(odd, got_ref[source, place, :], other_ref[source, place, :])
            rows.extend([south, low_ref[source, place, :], high_ref[source, place, :], north])
        turned = jnp.transpose(jnp.concatenate(rows, 0))
        mid_ref[plane] = turned
        first_ref[plane], second_ref[plane] = by_parity(
            odd_lon, turned[0:RIM], turned[turned.shape[0] - RIM :]
        )


def at(index):
    return slice(index * SUB, (index + 1) * SUB)


def weave_kernel(flags_ref, mid_ref, got_ref, other_ref, north_ref, east_face_ref, scale_ref, wide_ref):
    cols = mid_ref.shape[1]
    length = cols + 2 * RIM
    count = length // SUB
    for plane in range(mid_ref.shape[0]):
        west, east = by_parity(flags_ref[3:4, :] == 1, got_ref[plane], other_ref[plane])
        wide_ref[plane, 0:RIM, :] = west
        wide_ref[plane, RIM : RIM + cols, :] = mid_ref[plane]
        wide_ref[plane, RIM + cols :, :] = east
    for kind, target in enumerate((north_ref, east_face_ref, scale_ref)):
        for step in range(STEP):
            for j in range(count):
                target[at(j * STEP + step), :] = wide_ref[
                    kind * STEP + step, pl.ds(j, SUB, stride=count), :
                ]


def solve_kernel(
    flags_ref,
    north_ref,
    east_ref,
    scale_ref,
    mid_ref,
    got_ref,
    other_ref,
    lam_ref,
    image_ref,
    image_next_ref,
    seen_ref,
    seen_next_ref,
    parts_ref,
    u_ref,
    wide_ref,
    omega_ref,
    rhs_ref,
    turn_ref,
    t_ref,
    line_ref,
):
    cols = mid_ref.shape[1]
    length = cols + 2 * RIM
    count = length // SUB
    total = count * STEP
    lam = lam_ref[...]
    sub = iota((SUB, LANES), 0)
    lane = iota((SUB, LANES), 1)
    group = lane // REACH
    inner = (lane % REACH >= RIM // STEP) & (lane % REACH < REACH - RIM // STEP)
    for plane in range(2):
        west, east = by_parity(flags_ref[3:4, :] == 1, got_ref[plane], other_ref[plane])
        wide_ref[plane, 0:RIM, :] = west
        wide_ref[plane, RIM : RIM + cols, :] = mid_ref[plane]
        wide_ref[plane, RIM + cols :, :] = east

    def replicate(x):
        even = jnp.where(group % 2 == 0, x, pltpu.roll(x, REACH, 1))
        odd = jnp.where(group % 2 == 1, x, pltpu.roll(x, LANES - REACH, 1))
        even_far, odd_far = pltpu.roll(even, 2 * REACH, 1), pltpu.roll(odd, 2 * REACH, 1)
        near = group < 2
        return [
            jnp.where(near, even, even_far),
            jnp.where(near, odd, odd_far),
            jnp.where(near, even_far, even),
            jnp.where(near, odd_far, odd),
        ]

    def fold(x):
        near, centre, even = group < 2, (group == 1) | (group == 2), group % 2 == 0
        first = jnp.where(near, x[0], x[2]) + pltpu.roll(jnp.where(near, x[2], x[0]), 2 * REACH, 1)
        second = jnp.where(centre, x[1], x[3]) + pltpu.roll(jnp.where(centre, x[3], x[1]), 2 * REACH, 1)
        turned = pltpu.roll(jnp.where(even, second, first), LANES - REACH, 1)
        return jnp.where(even, first, second) + turned

    steps = range(STEP)

    def load(ref, j):
        return [ref[at(j * STEP + step), :] for step in steps]

    def across(j, here, ahead):
        face = load(east_ref, j)
        return [face[step] * (ahead[step] - here[step]) for step in steps]

    def seam_of(here, first):
        return across(count - 1, here, [pltpu.roll(x, SUB - 1, 0) for x in first])

    def advance(j, here, flux, west):
        face = load(north_ref, j)
        above = here[1:] + [pltpu.roll(here[0], LANES - 1, 1)]
        rise = [face[step] * (above[step] - here[step]) for step in steps]
        below = [pltpu.roll(rise[STEP - 1], 1, 1)] + rise[:-1]
        return [here[step] + ((flux[step] - west[step]) + (rise[step] - below[step])) for step in steps]

    def save(j, values):
        for step in steps:
            u_ref[at(j * STEP + step), :] = values[step]

    def diffuse():
        def two_passes(index, carry):
            here = load(u_ref, 0)
            seam = seam_of(load(u_ref, count - 1), here)
            west = [pltpu.roll(flux, 1, 0) for flux in seam]
            before = start = behind = None
            for j in range(count):
                if j + 1 < count:
                    ahead = load(u_ref, j + 1)
                    flux = across(j, here, ahead)
                else:
                    ahead, flux = here, seam
                after = advance(j, here, flux, west)
                west, here = flux, ahead
                if j == 0:
                    save(0, after)
                else:
                    cross = across(j - 1, before, after)
                    if j == 1:
                        start = cross
                    else:
                        save(j - 1, advance(j - 1, before, cross, behind))
                    behind = cross
                before = after
            first = load(u_ref, 0)
            seam = seam_of(before, first)
            save(count - 1, advance(count - 1, before, seam, behind))
            save(0, advance(0, first, start, [pltpu.roll(flux, 1, 0) for flux in seam]))
            return carry

        lax.fori_loop(0, PASSES // 2, two_passes, 0)

    zero = jnp.zeros((SUB, LANES), F32)
    own = [
        inner & (count * sub + j >= RIM) & (count * sub + j < RIM + cols) for j in range(count)
    ]
    spans = {}
    for j in range(count):
        edges = tuple(RIM <= count * row + j < RIM + cols for row in range(SUB))
        spans.setdefault(edges, []).append(j)

    kind_of = {j: edges for edges, members in spans.items() for j in members}

    def tally():
        return {edges: zero for edges in spans}

    def whole(sums):
        out = zero
        for edges, members in spans.items():
            out = out + jnp.where(own[members[0]], sums[edges], 0.0)
        return jnp.sum(jnp.sum(out, axis=1, keepdims=True), axis=0, keepdims=True)

    def ratio(top, bottom):
        return jnp.where(bottom > 0, top / jnp.where(bottom > 0, bottom, 1.0), 0.0)

    sum_bb, sum_bw, sum_00, sum_01 = tally(), tally(), tally(), tally()
    for j in range(count):
        omega_ref[at(j), :] = wide_ref[1, pl.ds(j, SUB, stride=count), :]
        spread = replicate(wide_ref[0, pl.ds(j, SUB, stride=count), :])
        for step in range(STEP):
            index = j * STEP + step
            u_ref[at(index), :] = lam * scale_ref[at(index), :] * spread[step]
    diffuse()
    for index in range(total):
        rhs = u_ref[at(index), :]
        rhs_ref[at(index), :] = rhs
        sum_bb[kind_of[index // STEP]] += rhs * rhs
    diffuse()
    for j in range(count):
        terms = []
        for index in range(j * STEP, (j + 1) * STEP):
            image = scale_ref[at(index), :] * u_ref[at(index), :]
            image_ref[at(index), :] = image
            terms.append(lam * image)
        seen = fold(terms)
        weighted = omega_ref[at(j), :] * seen
        t_ref[0, at(j), :] = seen
        sum_00[kind_of[j]] += weighted * seen
        spread = replicate(weighted)
        for step in range(STEP):
            index = j * STEP + step
            u_ref[at(index), :] = lam * scale_ref[at(index), :] * spread[step]
    diffuse()
    for index in range(total):
        turn = u_ref[at(index), :]
        turn_ref[at(index), :] = turn
        sum_bw[kind_of[index // STEP]] += turn * rhs_ref[at(index), :]
    diffuse()
    for j in range(count):
        terms = []
        for index in range(j * STEP, (j + 1) * STEP):
            image = scale_ref[at(index), :] * u_ref[at(index), :]
            image_next_ref[at(index), :] = image
            terms.append(lam * image)
        seen = fold(terms)
        t_ref[1, at(j), :] = seen
        sum_01[kind_of[j]] += omega_ref[at(j), :] * t_ref[0, at(j), :] * seen
    bb, bw, s00, s01 = whole(sum_bb), whole(sum_bw), whole(sum_00), whole(sum_01)
    fit, seen_fit = ratio(bw, bb), ratio(s01, s00)
    left, seen_left = tally(), tally()
    for index in range(total):
        gap = turn_ref[at(index), :] - fit * rhs_ref[at(index), :]
        left[kind_of[index // STEP]] += gap * gap
    for j in range(count):
        gap = t_ref[1, at(j), :] - seen_fit * t_ref[0, at(j), :]
        seen_left[kind_of[j]] += omega_ref[at(j), :] * (gap * gap)
    rest, seen_rest = whole(left), whole(seen_left)
    wide = iota(parts_ref.shape, 1)
    parts = jnp.zeros(parts_ref.shape, F32)
    for position, number in enumerate((bb, s00, bw, s01, fit, seen_fit, rest, seen_rest)):
        parts = jnp.where(wide == position, number, parts)
    parts_ref[...] = parts
    edge = RIM // STEP
    for plane, target in enumerate((seen_ref, seen_next_ref)):
        for j in range(count):
            line_ref[pl.ds(j, SUB, stride=count), :] = t_ref[plane, at(j), :]
        flat = jnp.transpose(line_ref[RIM : RIM + cols, :])
        depth = REACH - 2 * edge
        for step in range(STEP):
            start = step * REACH + edge
            target[step * depth : (step + 1) * depth, :] = flat[start : start + depth]


def pack_kernel(seen_ref, seen_next_ref, ids_ref, both_ref):
    rows = seen_ref.shape[0]
    blocks = ids_ref.shape[0]
    upper, lower = split(jnp.concatenate([seen_ref[...], seen_next_ref[...]], 1))
    both = jnp.concatenate([upper, lower], 0)
    ids = jnp.transpose(jnp.concatenate([ids_ref[...]] * (LANES // blocks), 0)).astype(jnp.int32)
    line = iota((LANES, 2 * rows), 1) % rows
    depth = rows // STEP
    wide = STEP * (line % depth) + line // depth + 1
    hot = jnp.concatenate(
        [(ids[:, block : block + 1] == wide).astype(F32).astype(BF16) for block in range(blocks)], 0
    )
    both_ref[...] = jnp.dot(hot, both, preferred_element_type=F32)


def answer_kernel(parts_ref, both_ref, back_ref, coef_ref):
    parts = parts_ref[...]

    def ahead(x, count):
        return pltpu.roll(x, LANES - count, 1)

    def add(x):
        return jnp.broadcast_to(jnp.sum(x, axis=0, keepdims=True), (SUB, LANES))

    sums = add(parts)
    fits = jnp.where(sums > 0, ahead(sums, 2) / sums, 0.0)
    gap = ahead(parts, 4) - fits[0:1, :]
    rests = add(ahead(parts, 6) + gap * (gap * parts))

    def pick(x, lane):
        return x[0:1, lane : lane + 1]

    bb, s00, bw = pick(sums, 0), pick(sums, 1), pick(sums, 2)
    fit, seen_fit = pick(fits, 0), pick(fits, 1)
    rest, seen_rest = pick(rests, 0), pick(rests, 1)
    step = bb / (bb + bw)
    tilt = rest / (bb + bw)
    full = fit + tilt
    gap = seen_fit - full
    energy = rest + tilt * tilt * bb + seen_rest + gap * (gap * s00)
    step_next = jnp.where(rest > 0, rest / jnp.where(rest > 0, energy, 1.0), 0.0)
    coef = step * (1.0 + step_next * full)
    coef_next = -step * step_next
    line = iota(coef_ref.shape, 0)
    coef_ref[...] = jnp.where(line == 0, coef, coef_next)
    back_ref[...] = coef * both_ref[:, 0:LANES] + coef_next * both_ref[:, LANES:]


def increment_kernel(image_ref, image_next_ref, coef_ref, out_ref, line_ref):
    fields, _, cols = out_ref.shape
    count = image_ref.shape[0] // (SUB * STEP)
    coef, coef_next = coef_ref[0:1, :], coef_ref[1:2, :]
    edge = RIM // STEP
    depth = REACH - 2 * edge
    for step in range(STEP):
        for j in range(count):
            index = at(j * STEP + step)
            line_ref[step, pl.ds(j, SUB, stride=count), :] = (
                coef * image_ref[index, :] + coef_next * image_next_ref[index, :]
            )
        flat = jnp.transpose(line_ref[step, RIM : RIM + cols, :])
        for field in range(fields):
            start = field * REACH + edge
            out_ref[field, pl.ds(step, depth, stride=STEP), :] = flat[start : start + depth]


def depart_kernel(back_ref, slot_ref, off_ref, inn_ref, out_ref):
    slots = back_ref.shape[0]
    upper, lower = split(back_ref[...])
    slot = slot_ref[...].astype(jnp.int32)
    line = iota((LANES, LANES), 1)
    place = jnp.concatenate(
        [
            jnp.concatenate(
                [
                    (slot[block * LANES : (block + 1) * LANES] == line + part * LANES).astype(F32).astype(BF16)
                    for part in range(slots // LANES)
                ],
                1,
            )
            for block in range(slot.shape[0] // LANES)
        ],
        0,
    )
    rows = jnp.dot(place, jnp.concatenate([upper, lower], 1), preferred_element_type=F32)
    seen = jnp.take_along_axis(rows[:, 0:LANES] + rows[:, LANES:], off_ref[...], axis=1)
    out_ref[...] = inn_ref[...] - seen


def swap(first, second, axis, periodic):
    count = lax.axis_size(axis)
    pairs = [[(i, i + 1) for i in range(start, count - 1, 2)] for start in (0, 1)]
    if periodic:
        pairs[1].append((count - 1, 0))
    both = [edges + [(target, source) for source, target in edges] for edges in pairs]
    return lax.ppermute(first, axis, both[0]), lax.ppermute(second, axis, both[1])


def exchange(flags, low, high, first, second, order):
    planes = len(order)
    got, other = swap(first, second, "lat", False)
    mid, first, second = call(
        functools.partial(turn_kernel, order),
        [((planes, LANES, LANES), F32), ((planes, RIM, LANES), F32), ((planes, RIM, LANES), F32)],
        (flags, low, high, got, other),
        nbytes=4 * planes * 300 * LANES,
    )
    got, other = swap(first, second, "lon", True)
    return mid, got, other


def analyse(
    lat_coef, lon_coef, std_scale, land_mask, lst_weights, innovation, inv_var, owner, row_ids, offsets
):
    fields, tile_rows, tile_cols = lat_coef.shape
    tiles, width = innovation.shape
    lat_count, lon_count = lax.axis_size("lat"), lax.axis_size("lon")
    devices = lat_count * lon_count
    capacity = max(2, 2 * tiles // devices)
    if (fields * REACH, tile_cols, width, tile_rows + 2 * RIM) != (LANES,) * 4:
        raise ValueError("tile shape")
    if RIM > tile_rows // 2 or lat_count % 2 or lon_count % 2 or capacity % SUB or LANES % capacity or tiles % LANES:
        raise ValueError("slot shape")
    half = tile_rows // 2
    slots = devices * capacity
    lat_index, lon_index = lax.axis_index("lat"), lax.axis_index("lon")
    last = (lat_index == lat_count - 1).astype(jnp.int32)
    flags = jnp.zeros((SUB, LANES), jnp.int32)
    for line, flag in enumerate((last, lat_index * lon_count + lon_index, lat_index % 2, lon_index % 2)):
        flags = jnp.where(iota(flags.shape, 0) == line, flag.astype(jnp.int32), flags)

    tables = (owner.reshape(1, tiles), row_ids.reshape(1, tiles), innovation, inv_var, offsets)
    face_low, face_high, *rest = call(
        functools.partial(faces_kernel, fields),
        [((3 * fields, half, LANES), F32)] * 4 + [(x.shape, x.dtype) for x in tables],
        (flags, lat_coef, lon_coef, std_scale, land_mask) + tables,
        scratch=[pltpu.VMEM(x.shape, x.dtype) for x in (lat_coef, lon_coef, std_scale, land_mask)]
        + [pltpu.SemaphoreType.DMA((9,))],
        hbm=range(1, 10),
    )
    face_ends, tables = rest[0:2], rest[2:]
    block = 2 * capacity + 1
    send, slot = call(
        functools.partial(route_kernel, devices, capacity),
        [((devices * block, LANES), F32), ((tiles, LANES), F32)],
        (flags, *tables),
        scratch=[pltpu.VMEM((tiles, 2 * LANES), F32), pltpu.VMEM((slots, 2 * LANES), F32)],
        flops=10**9,
        nbytes=10**7,
    )
    face_all = exchange(
        flags,
        face_low,
        face_high,
        *face_ends,
        [[(kind * fields + field, step) for field in range(fields)] for kind in range(3) for step in range(STEP)],
    )
    got = lax.all_to_all(
        send.reshape(devices, 1, block * LANES), AXES, split_axis=0, concat_axis=0, tiled=True
    ).reshape(devices * block, LANES)
    span = tile_cols + 2 * RIM
    woven = (span * STEP, LANES)
    north8, east8, scale8 = call(
        weave_kernel,
        [(woven, F32)] * 3,
        (flags, *face_all),
        scratch=(pltpu.VMEM((3 * STEP, span, LANES), F32),),
        nbytes=3 * 10**6,
    )
    low, high, ids, *ends = call(
        functools.partial(collect_kernel, devices, capacity),
        [((2, half, LANES), F32)] * 2 + [((slots // LANES, LANES), F32)] + [((2, half, LANES), F32)] * 2,
        (flags, got),
    )
    grid = exchange(flags, low, high, *ends, [[(plane, step) for step in range(STEP)] for plane in range(2)])
    lam = jnp.broadcast_to(jnp.repeat(lst_weights, REACH)[None, :], (SUB, LANES))
    image, image_next, seen, seen_next, parts = call(
        solve_kernel,
        [(woven, F32)] * 2 + [((tile_rows, LANES), F32)] * 2 + [((devices, LANES), F32)],
        (flags, north8, east8, scale8, *grid, lam),
        scratch=(
            pltpu.VMEM(woven, F32),
            pltpu.VMEM((2, span, LANES), F32),
            pltpu.VMEM((span, LANES), F32),
            pltpu.VMEM(woven, F32),
            pltpu.VMEM(woven, F32),
            pltpu.VMEM((2, span, LANES), F32),
            pltpu.VMEM((span, LANES), F32),
        ),
        flops=10**9,
        nbytes=10**7,
    )
    (both,) = call(pack_kernel, [((slots, 2 * LANES), F32)], (seen, seen_next, ids), nbytes=10**6)
    parts = lax.all_to_all(parts, AXES, split_axis=0, concat_axis=0, tiled=True)
    back, coef = call(
        answer_kernel, [((slots, LANES), F32), ((SUB, LANES), F32)], (parts, both), nbytes=10**6
    )
    back = lax.all_to_all(
        back.reshape(devices, capacity, LANES), AXES, split_axis=0, concat_axis=0, tiled=True
    ).reshape(slots, LANES)
    (increment,) = call(
        increment_kernel,
        [((fields, tile_rows, tile_cols), F32)],
        (image, image_next, coef),
        scratch=(pltpu.VMEM((STEP, span, LANES), F32),),
        nbytes=10**6,
    )
    (departure,) = call(depart_kernel, [((tiles, width), F32)], (back, slot, tables[4], tables[2]))
    return increment, departure


def solution(mesh):
    grid = P(None, "lat", "lon")
    tile = P(AXES, None)
    in_specs = (grid, grid, grid, P("lat", "lon"), P(), tile, tile, tile, P(AXES), tile)
    return jax.shard_map(analyse, mesh=mesh, in_specs=in_specs, out_specs=(grid, tile), check_vma=False)
```

```python
import functools

import jax
import jax.numpy as jnp
from jax import lax
from jax.experimental import pallas as pl
from jax.experimental.pallas import tpu as pltpu
from jax.sharding import PartitionSpec as P

PASSES = 8
RIM = 4 * PASSES
LANES = 128
SUB = 8
GROUP = 8
STEP = 4
REACH = LANES // STEP
LOW_BITS = 5
LOW = 2**LOW_BITS
AXES = ("lat", "lon")
F32 = jnp.float32
BF16 = jnp.bfloat16


def iota(shape, dim):
    return lax.broadcasted_iota(jnp.int32, shape, dim)


def call(kernel, outs, args, scratch=(), hbm=(), flops=1000, nbytes=100000):
    spaces = [pltpu.VMEM] * len(args)
    for index in hbm:
        spaces[index] = pltpu.HBM
    args = [
        pltpu.with_memory_space_constraint(arg, pltpu.HBM) if space == pltpu.HBM else arg
        for arg, space in zip(args, spaces)
    ]
    return pl.pallas_call(
        kernel,
        out_shape=[jax.ShapeDtypeStruct(shape, dtype) for shape, dtype in outs],
        in_specs=[pl.BlockSpec(memory_space=space) for space in spaces],
        out_specs=[pl.BlockSpec(memory_space=pltpu.VMEM)] * len(outs),
        scratch_shapes=list(scratch),
        compiler_params=pltpu.CompilerParams(vmem_limit_bytes=20 * 2**20),
        cost_estimate=pl.CostEstimate(flops=flops, bytes_accessed=nbytes, transcendentals=0),
    )(*args)


def fetch(sources, targets, sems):
    copies = [
        pltpu.make_async_copy(source, target, sems.at[index])
        for index, (source, target) in enumerate(zip(sources, targets))
    ]
    for copy in copies:
        copy.start()
    return copies


def split(value):
    high = value.astype(BF16)
    low = (value - high.astype(F32)).astype(BF16)
    return high, low


def contract(left, right, dims):
    return lax.dot_general(left, right, (dims, ((), ())), preferred_element_type=F32)


def swap_blocks(x, sub, lane):
    block = lane // LOW
    own = sub % 4
    up = pltpu.roll(pltpu.roll(x, SUB - 1, 0), LOW, 1)
    down = pltpu.roll(pltpu.roll(x, 1, 0), LANES - LOW, 1)
    odd_row, odd_block = own % 2, block % 2
    x = jnp.where(odd_row == odd_block, x, jnp.where(odd_row == 0, up, down))
    turned = pltpu.roll(x, 2 * LOW, 1)
    up = pltpu.roll(turned, SUB - 2, 0)
    down = pltpu.roll(turned, 2, 0)
    high_row, high_block = own // 2, block // 2
    return jnp.where(high_row == high_block, x, jnp.where(high_row == 0, up, down))


def route_kernel(devices, capacity, *refs):
    flags_ref, sources = refs[0], refs[1:6]
    send_ref, slot_ref, rows_ref, packed_ref = refs[6:10]
    owner_ref, rid_ref, inn_ref, var_ref, off_ref = sources
    tiles = off_ref.shape[0]
    per_row = LANES // capacity
    hits = (owner_ref[...] == iota((devices, tiles), 0)).astype(F32)
    earlier = (iota((tiles, tiles), 0) < iota((tiles, tiles), 1)).astype(F32).astype(BF16)
    before = jnp.dot(hits.astype(BF16), earlier, preferred_element_type=F32)
    rank = jnp.sum(hits * before, axis=0, keepdims=True)
    slot_row = owner_ref[...] * capacity + rank.astype(jnp.int32)
    slot_ref[...] = jnp.transpose(jnp.broadcast_to(slot_row.astype(F32), (LANES, tiles)))
    shift = (flags_ref[1:2, 0:1] % per_row) * capacity
    rank_hot = (rank.astype(jnp.int32) + shift == iota((LANES, tiles), 0)).astype(F32).astype(BF16)
    marked = hits * (rid_ref[...].astype(F32) + 1.0)
    ids = contract(marked.astype(BF16), rank_hot, ((1,), (1,)))
    block = 2 * capacity + 1
    for device in range(devices):
        place = device * block + 2 * capacity
        send_ref[place : place + 1, :] = ids[device : device + 1, :]
    sub = iota((SUB, LANES), 0)
    lane = iota((SUB, LANES), 1)
    tall = iota((LOW, LANES), 0)

    def expand(index, carry):
        start = pl.multiple_of(index * GROUP, GROUP)
        window = pl.ds(start, GROUP)
        offsets = off_ref[window, :]
        weight = var_ref[window, :]
        value = weight * inn_ref[window, :]
        low = offsets & (LOW - 1)
        high = offsets >> LOW_BITS
        hot, parts = [], []
        for tile in range(GROUP):
            pick = slice(tile, tile + 1)
            hot.append((low[pick, :] == tall).astype(F32).astype(BF16))
            both = jnp.where(sub < 4, value[pick, :], weight[pick, :])
            parts.append(jnp.where(high[pick, :] == sub % 4, both, 0.0))
        upper, lower = split(jnp.concatenate(parts, 0))
        product = contract(jnp.concatenate([upper, lower], 0), jnp.concatenate(hot, 0), ((1,), (1,)))
        half = GROUP * SUB
        total = product[:half] + product[half:]
        quads = []
        for side in range(2):
            lanes = slice(side * LANES, (side + 1) * LANES)
            merged = total[side * 4 * SUB : (side * 4 + 1) * SUB, lanes]
            for tile in range(1, 4):
                base = (side * 4 + tile) * SUB
                merged = jnp.where(lane // LOW == tile, total[base : base + SUB, lanes], merged)
            quads.append(swap_blocks(merged, sub, lane))
        first, second = quads
        rows_ref[window, 0:LANES] = jnp.where(sub < 4, first, pltpu.roll(second, 4, 0))
        rows_ref[window, LANES : 2 * LANES] = jnp.where(sub < 4, pltpu.roll(first, 4, 0), second)
        return carry

    lax.fori_loop(0, tiles // GROUP, expand, 0, unroll=64)
    upper, lower = split(rows_ref[...])
    slots = devices * capacity
    place = (iota((slots, tiles), 0) == slot_row).astype(F32).astype(BF16)
    packed_ref[...] = jnp.dot(place, upper, preferred_element_type=F32)
    packed_ref[...] += jnp.dot(place, lower, preferred_element_type=F32)
    for device in range(devices):
        for side in range(2):
            start = device * block + side * capacity
            send_ref[start : start + capacity, :] = packed_ref[
                device * capacity : (device + 1) * capacity, side * LANES : (side + 1) * LANES
            ]


def by_parity(odd, low, high):
    return jnp.where(odd, low, high), jnp.where(odd, high, low)


def collect_kernel(devices, capacity, flags_ref, got_ref, low_ref, high_ref, ids_ref, first_ref, second_ref):
    block = 2 * capacity + 1
    per_row = LANES // capacity
    rows = 2 * low_ref.shape[1]
    total = jnp.zeros((rows, 2 * LANES), F32)
    line = iota((rows, LANES), 0)
    tall = line // RIM * RIM + STEP * (line % SUB) + line % RIM // SUB + 1

    def piece(device, start, size):
        return got_ref[device * block + start : device * block + start + size, :]

    for group in range(devices // per_row):
        members = range(group * per_row, (group + 1) * per_row)
        ids = sum(piece(device, 2 * capacity, 1) for device in members)
        ids_ref[group : group + 1, :] = ids
        hot = (ids.astype(jnp.int32) == tall).astype(F32).astype(BF16)
        values = jnp.concatenate(
            [
                jnp.concatenate([piece(device, side * capacity, capacity) for device in members], 0)
                for side in range(2)
            ],
            1,
        )
        upper, lower = split(values)
        total = total + contract(
            jnp.concatenate([hot, hot], 1), jnp.concatenate([upper, lower], 0), ((1,), (0,))
        )
    half = rows // 2
    odd = flags_ref[2:3, :] == 1
    for plane in range(2):
        lanes = slice(plane * LANES, (plane + 1) * LANES)
        low, high = total[0:half, lanes], total[half:, lanes]
        low_ref[plane] = low
        high_ref[plane] = high
        first_ref[plane], second_ref[plane] = by_parity(odd, low, high)


def faces_kernel(fields, flags_ref, *refs):
    low_ref, high_ref, first_ref, second_ref = refs[9:13]
    lat_ref, lon_ref, std_ref, mask_ref = local = refs[18:22]
    copies = fetch(refs[0:9], local + refs[13:18], refs[22])
    for copy in copies[0:4]:
        copy.wait()
    final = (iota((SUB, LANES), 0) == SUB - 1) & (flags_ref[0:1, :] == 1)
    for part, target in enumerate((low_ref, high_ref)):
        for step in range(STEP):
            rows = pl.ds(part * RIM + step, SUB, stride=STEP)
            place = slice(step * SUB, (step + 1) * SUB)
            mask = mask_ref[rows, :].astype(F32)
            for field in range(fields):
                face = lat_ref[field, rows, :]
                if part == 1 and step == STEP - 1:
                    face = jnp.where(final, 0.0, face)
                target[field, place, :] = face
                target[fields + field, place, :] = lon_ref[field, rows, :]
                target[2 * fields + field, place, :] = mask * std_ref[field, rows, :]
    odd = flags_ref[2:3, :] == 1
    for plane in range(3 * fields):
        first_ref[plane], second_ref[plane] = by_parity(odd, low_ref[plane], high_ref[plane])
    for copy in copies[4:]:
        copy.wait()


def turn_kernel(order, flags_ref, low_ref, high_ref, got_ref, other_ref, mid_ref, first_ref, second_ref):
    odd = flags_ref[2:3, :] == 1
    odd_lon = flags_ref[3:4, :] == 1
    for plane, pieces in enumerate(order):
        rows = []
        for source, step in pieces:
            place = slice(step * SUB, (step + 1) * SUB)
            south, north = by_parity(odd, got_ref[source, place, :], other_ref[source, place, :])
            rows.extend([south, low_ref[source, place, :], high_ref[source, place, :], north])
        turned = jnp.transpose(jnp.concatenate(rows, 0))
        mid_ref[plane] = turned
        first_ref[plane], second_ref[plane] = by_parity(
            odd_lon, turned[0:RIM], turned[turned.shape[0] - RIM :]
        )


def at(index):
    return slice(index * SUB, (index + 1) * SUB)


def weave_kernel(flags_ref, mid_ref, got_ref, other_ref, north_ref, east_face_ref, scale_ref, wide_ref):
    cols = mid_ref.shape[1]
    length = cols + 2 * RIM
    count = length // SUB
    for plane in range(mid_ref.shape[0]):
        west, east = by_parity(flags_ref[3:4, :] == 1, got_ref[plane], other_ref[plane])
        wide_ref[plane, 0:RIM, :] = west
        wide_ref[plane, RIM : RIM + cols, :] = mid_ref[plane]
        wide_ref[plane, RIM + cols :, :] = east
    for kind, target in enumerate((north_ref, east_face_ref, scale_ref)):
        for step in range(STEP):
            for j in range(count):
                target[at(j * STEP + step), :] = wide_ref[
                    kind * STEP + step, pl.ds(j, SUB, stride=count), :
                ]


def solve_kernel(
    flags_ref,
    north_ref,
    east_ref,
    scale_ref,
    mid_ref,
    got_ref,
    other_ref,
    lam_ref,
    image_ref,
    image_next_ref,
    seen_ref,
    seen_next_ref,
    parts_ref,
    u_ref,
    wide_ref,
    omega_ref,
    rhs_ref,
    turn_ref,
    t_ref,
    line_ref,
):
    cols = mid_ref.shape[1]
    length = cols + 2 * RIM
    count = length // SUB
    total = count * STEP
    lam = lam_ref[...]
    sub = iota((SUB, LANES), 0)
    lane = iota((SUB, LANES), 1)
    group = lane // REACH
    inner = (lane % REACH >= RIM // STEP) & (lane % REACH < REACH - RIM // STEP)
    for plane in range(2):
        west, east = by_parity(flags_ref[3:4, :] == 1, got_ref[plane], other_ref[plane])
        wide_ref[plane, 0:RIM, :] = west
        wide_ref[plane, RIM : RIM + cols, :] = mid_ref[plane]
        wide_ref[plane, RIM + cols :, :] = east

    def replicate(x):
        even = jnp.where(group % 2 == 0, x, pltpu.roll(x, REACH, 1))
        odd = jnp.where(group % 2 == 1, x, pltpu.roll(x, LANES - REACH, 1))
        even_far, odd_far = pltpu.roll(even, 2 * REACH, 1), pltpu.roll(odd, 2 * REACH, 1)
        near = group < 2
        return [
            jnp.where(near, even, even_far),
            jnp.where(near, odd, odd_far),
            jnp.where(near, even_far, even),
            jnp.where(near, odd_far, odd),
        ]

    def fold(x):
        near, centre, even = group < 2, (group == 1) | (group == 2), group % 2 == 0
        first = jnp.where(near, x[0], x[2]) + pltpu.roll(jnp.where(near, x[2], x[0]), 2 * REACH, 1)
        second = jnp.where(centre, x[1], x[3]) + pltpu.roll(jnp.where(centre, x[3], x[1]), 2 * REACH, 1)
        turned = pltpu.roll(jnp.where(even, second, first), LANES - REACH, 1)
        return jnp.where(even, first, second) + turned

    steps = range(STEP)

    def load(ref, j):
        return [ref[at(j * STEP + step), :] for step in steps]

    def across(j, here, ahead):
        face = load(east_ref, j)
        return [face[step] * (ahead[step] - here[step]) for step in steps]

    def seam_of(here, first):
        return across(count - 1, here, [pltpu.roll(x, SUB - 1, 0) for x in first])

    def advance(j, here, flux, west):
        face = load(north_ref, j)
        above = here[1:] + [pltpu.roll(here[0], LANES - 1, 1)]
        rise = [face[step] * (above[step] - here[step]) for step in steps]
        below = [pltpu.roll(rise[STEP - 1], 1, 1)] + rise[:-1]
        return [here[step] + ((flux[step] - west[step]) + (rise[step] - below[step])) for step in steps]

    def save(j, values):
        for step in steps:
            u_ref[at(j * STEP + step), :] = values[step]

    def diffuse():
        def two_passes(index, carry):
            here = load(u_ref, 0)
            seam = seam_of(load(u_ref, count - 1), here)
            west = [pltpu.roll(flux, 1, 0) for flux in seam]
            before = start = behind = None
            for j in range(count):
                if j + 1 < count:
                    ahead = load(u_ref, j + 1)
                    flux = across(j, here, ahead)
                else:
                    ahead, flux = here, seam
                after = advance(j, here, flux, west)
                west, here = flux, ahead
                if j == 0:
                    save(0, after)
                else:
                    cross = across(j - 1, before, after)
                    if j == 1:
                        start = cross
                    else:
                        save(j - 1, advance(j - 1, before, cross, behind))
                    behind = cross
                before = after
            first = load(u_ref, 0)
            seam = seam_of(before, first)
            save(count - 1, advance(count - 1, before, seam, behind))
            save(0, advance(0, first, start, [pltpu.roll(flux, 1, 0) for flux in seam]))
            return carry

        lax.fori_loop(0, PASSES // 2, two_passes, 0)

    zero = jnp.zeros((SUB, LANES), F32)
    own = [
        inner & (count * sub + j >= RIM) & (count * sub + j < RIM + cols) for j in range(count)
    ]
    spans = {}
    for j in range(count):
        edges = tuple(RIM <= count * row + j < RIM + cols for row in range(SUB))
        spans.setdefault(edges, []).append(j)

    kind_of = {j: edges for edges, members in spans.items() for j in members}

    def tally():
        return {edges: zero for edges in spans}

    def whole(sums):
        out = zero
        for edges, members in spans.items():
            out = out + jnp.where(own[members[0]], sums[edges], 0.0)
        return jnp.sum(jnp.sum(out, axis=1, keepdims=True), axis=0, keepdims=True)

    def ratio(top, bottom):
        return jnp.where(bottom > 0, top / jnp.where(bottom > 0, bottom, 1.0), 0.0)

    sum_bb, sum_bw, sum_00, sum_01 = tally(), tally(), tally(), tally()
    for j in range(count):
        omega_ref[at(j), :] = wide_ref[1, pl.ds(j, SUB, stride=count), :]
        spread = replicate(wide_ref[0, pl.ds(j, SUB, stride=count), :])
        for step in range(STEP):
            index = j * STEP + step
            u_ref[at(index), :] = lam * scale_ref[at(index), :] * spread[step]
    diffuse()
    for index in range(total):
        rhs = u_ref[at(index), :]
        rhs_ref[at(index), :] = rhs
        sum_bb[kind_of[index // STEP]] += rhs * rhs
    diffuse()
    for j in range(count):
        terms = []
        for index in range(j * STEP, (j + 1) * STEP):
            image = scale_ref[at(index), :] * u_ref[at(index), :]
            image_ref[at(index), :] = image
            terms.append(lam * image)
        seen = fold(terms)
        weighted = omega_ref[at(j), :] * seen
        t_ref[0, at(j), :] = seen
        sum_00[kind_of[j]] += weighted * seen
        spread = replicate(weighted)
        for step in range(STEP):
            index = j * STEP + step
            u_ref[at(index), :] = lam * scale_ref[at(index), :] * spread[step]
    diffuse()
    for index in range(total):
        turn = u_ref[at(index), :]
        turn_ref[at(index), :] = turn
        sum_bw[kind_of[index // STEP]] += turn * rhs_ref[at(index), :]
    diffuse()
    for j in range(count):
        terms = []
        for index in range(j * STEP, (j + 1) * STEP):
            image = scale_ref[at(index), :] * u_ref[at(index), :]
            image_next_ref[at(index), :] = image
            terms.append(lam * image)
        seen = fold(terms)
        t_ref[1, at(j), :] = seen
        sum_01[kind_of[j]] += omega_ref[at(j), :] * t_ref[0, at(j), :] * seen
    bb, bw, s00, s01 = whole(sum_bb), whole(sum_bw), whole(sum_00), whole(sum_01)
    fit, seen_fit = ratio(bw, bb), ratio(s01, s00)
    left, seen_left = tally(), tally()
    for index in range(total):
        gap = turn_ref[at(index), :] - fit * rhs_ref[at(index), :]
        left[kind_of[index // STEP]] += gap * gap
    for j in range(count):
        gap = t_ref[1, at(j), :] - seen_fit * t_ref[0, at(j), :]
        seen_left[kind_of[j]] += omega_ref[at(j), :] * (gap * gap)
    rest, seen_rest = whole(left), whole(seen_left)
    wide = iota(parts_ref.shape, 1)
    parts = jnp.zeros(parts_ref.shape, F32)
    for position, number in enumerate((bb, s00, bw, s01, fit, seen_fit, rest, seen_rest)):
        parts = jnp.where(wide == position, number, parts)
    parts_ref[...] = parts
    edge = RIM // STEP
    for plane, target in enumerate((seen_ref, seen_next_ref)):
        for j in range(count):
            line_ref[pl.ds(j, SUB, stride=count), :] = t_ref[plane, at(j), :]
        flat = jnp.transpose(line_ref[RIM : RIM + cols, :])
        depth = REACH - 2 * edge
        for step in range(STEP):
            start = step * REACH + edge
            target[step * depth : (step + 1) * depth, :] = flat[start : start + depth]


def pack_kernel(seen_ref, seen_next_ref, ids_ref, both_ref):
    rows = seen_ref.shape[0]
    blocks = ids_ref.shape[0]
    upper, lower = split(jnp.concatenate([seen_ref[...], seen_next_ref[...]], 1))
    both = jnp.concatenate([upper, lower], 0)
    ids = jnp.transpose(jnp.concatenate([ids_ref[...]] * (LANES // blocks), 0)).astype(jnp.int32)
    line = iota((LANES, 2 * rows), 1) % rows
    depth = rows // STEP
    wide = STEP * (line % depth) + line // depth + 1
    hot = jnp.concatenate(
        [(ids[:, block : block + 1] == wide).astype(F32).astype(BF16) for block in range(blocks)], 0
    )
    both_ref[...] = jnp.dot(hot, both, preferred_element_type=F32)


def answer_kernel(parts_ref, both_ref, back_ref, coef_ref):
    parts = parts_ref[...]

    def ahead(x, count):
        return pltpu.roll(x, LANES - count, 1)

    def add(x):
        return jnp.broadcast_to(jnp.sum(x, axis=0, keepdims=True), (SUB, LANES))

    sums = add(parts)
    fits = jnp.where(sums > 0, ahead(sums, 2) / sums, 0.0)
    gap = ahead(parts, 4) - fits[0:1, :]
    rests = add(ahead(parts, 6) + gap * (gap * parts))

    def pick(x, lane):
        return x[0:1, lane : lane + 1]

    bb, s00, bw = pick(sums, 0), pick(sums, 1), pick(sums, 2)
    fit, seen_fit = pick(fits, 0), pick(fits, 1)
    rest, seen_rest = pick(rests, 0), pick(rests, 1)
    step = bb / (bb + bw)
    tilt = rest / (bb + bw)
    full = fit + tilt
    gap = seen_fit - full
    energy = rest + tilt * tilt * bb + seen_rest + gap * (gap * s00)
    step_next = jnp.where(rest > 0, rest / jnp.where(rest > 0, energy, 1.0), 0.0)
    coef = step * (1.0 + step_next * full)
    coef_next = -step * step_next
    line = iota(coef_ref.shape, 0)
    coef_ref[...] = jnp.where(line == 0, coef, coef_next)
    back_ref[...] = coef * both_ref[:, 0:LANES] + coef_next * both_ref[:, LANES:]


def increment_kernel(image_ref, image_next_ref, coef_ref, out_ref, line_ref):
    fields, _, cols = out_ref.shape
    count = image_ref.shape[0] // (SUB * STEP)
    coef, coef_next = coef_ref[0:1, :], coef_ref[1:2, :]
    edge = RIM // STEP
    depth = REACH - 2 * edge
    for step in range(STEP):
        for j in range(count):
            index = at(j * STEP + step)
            line_ref[step, pl.ds(j, SUB, stride=count), :] = (
                coef * image_ref[index, :] + coef_next * image_next_ref[index, :]
            )
        flat = jnp.transpose(line_ref[step, RIM : RIM + cols, :])
        for field in range(fields):
            start = field * REACH + edge
            out_ref[field, pl.ds(step, depth, stride=STEP), :] = flat[start : start + depth]


def depart_kernel(back_ref, slot_ref, off_ref, inn_ref, out_ref):
    slots = back_ref.shape[0]
    upper, lower = split(back_ref[...])
    slot = slot_ref[...].astype(jnp.int32)
    line = iota((LANES, LANES), 1)
    place = jnp.concatenate(
        [
            jnp.concatenate(
                [
                    (slot[block * LANES : (block + 1) * LANES] == line + part * LANES).astype(F32).astype(BF16)
                    for part in range(slots // LANES)
                ],
                1,
            )
            for block in range(slot.shape[0] // LANES)
        ],
        0,
    )
    rows = jnp.dot(place, jnp.concatenate([upper, lower], 1), preferred_element_type=F32)
    seen = jnp.take_along_axis(rows[:, 0:LANES] + rows[:, LANES:], off_ref[...], axis=1)
    out_ref[...] = inn_ref[...] - seen


def swap(first, second, axis, periodic):
    count = lax.axis_size(axis)
    pairs = [[(i, i + 1) for i in range(start, count - 1, 2)] for start in (0, 1)]
    if periodic:
        pairs[1].append((count - 1, 0))
    both = [edges + [(target, source) for source, target in edges] for edges in pairs]
    got = lax.ppermute(first, axis, both[0])
    other = lax.ppermute(second, axis, both[1])
    return got, other


def exchange(flags, low, high, first, second, order):
    planes = len(order)
    got, other = swap(first, second, "lat", False)
    mid, first, second = call(
        functools.partial(turn_kernel, order),
        [((planes, LANES, LANES), F32), ((planes, RIM, LANES), F32), ((planes, RIM, LANES), F32)],
        (flags, low, high, got, other),
        nbytes=4 * planes * 300 * LANES,
    )
    got, other = swap(first, second, "lon", True)
    return mid, got, other


def analyse(
    lat_coef, lon_coef, std_scale, land_mask, lst_weights, innovation, inv_var, owner, row_ids, offsets
):
    fields, tile_rows, tile_cols = lat_coef.shape
    tiles, width = innovation.shape
    lat_count, lon_count = lax.axis_size("lat"), lax.axis_size("lon")
    devices = lat_count * lon_count
    capacity = max(2, 2 * tiles // devices)
    if (fields * REACH, tile_cols, width, tile_rows + 2 * RIM) != (LANES,) * 4:
        raise ValueError("tile shape")
    if RIM > tile_rows // 2 or lat_count % 2 or lon_count % 2 or capacity % SUB or LANES % capacity or tiles % LANES:
        raise ValueError("slot shape")
    half = tile_rows // 2
    slots = devices * capacity
    lat_index, lon_index = lax.axis_index("lat"), lax.axis_index("lon")
    last = (lat_index == lat_count - 1).astype(jnp.int32)
    flags = jnp.zeros((SUB, LANES), jnp.int32)
    for line, flag in enumerate((last, lat_index * lon_count + lon_index, lat_index % 2, lon_index % 2)):
        flags = jnp.where(iota(flags.shape, 0) == line, flag.astype(jnp.int32), flags)

    tables = (owner.reshape(1, tiles), row_ids.reshape(1, tiles), innovation, inv_var, offsets)
    face_low, face_high, *rest = call(
        functools.partial(faces_kernel, fields),
        [((3 * fields, half, LANES), F32)] * 4 + [(x.shape, x.dtype) for x in tables],
        (flags, lat_coef, lon_coef, std_scale, land_mask) + tables,
        scratch=[pltpu.VMEM(x.shape, x.dtype) for x in (lat_coef, lon_coef, std_scale, land_mask)]
        + [pltpu.SemaphoreType.DMA((9,))],
        hbm=range(1, 10),
    )
    face_ends, tables = rest[0:2], rest[2:]
    block = 2 * capacity + 1
    send, slot = call(
        functools.partial(route_kernel, devices, capacity),
        [((devices * block, LANES), F32), ((tiles, LANES), F32)],
        (flags, *tables),
        scratch=[pltpu.VMEM((tiles, 2 * LANES), F32), pltpu.VMEM((slots, 2 * LANES), F32)],
        flops=10**9,
        nbytes=10**7,
    )
    face_all = exchange(
        flags,
        face_low,
        face_high,
        *face_ends,
        [[(kind * fields + field, step) for field in range(fields)] for kind in range(3) for step in range(STEP)],
    )
    got = lax.all_to_all(
        send.reshape(devices, 1, block * LANES), AXES, split_axis=0, concat_axis=0, tiled=True
    ).reshape(devices * block, LANES)
    span = tile_cols + 2 * RIM
    woven = (span * STEP, LANES)
    north8, east8, scale8 = call(
        weave_kernel,
        [(woven, F32)] * 3,
        (flags, *face_all),
        scratch=(pltpu.VMEM((3 * STEP, span, LANES), F32),),
        nbytes=3 * 10**6,
    )
    low, high, ids, *ends = call(
        functools.partial(collect_kernel, devices, capacity),
        [((2, half, LANES), F32)] * 2 + [((slots // LANES, LANES), F32)] + [((2, half, LANES), F32)] * 2,
        (flags, got),
    )
    grid = exchange(flags, low, high, *ends, [[(plane, step) for step in range(STEP)] for plane in range(2)])
    lam = jnp.broadcast_to(jnp.repeat(lst_weights, REACH)[None, :], (SUB, LANES))
    image, image_next, seen, seen_next, parts = call(
        solve_kernel,
        [(woven, F32)] * 2 + [((tile_rows, LANES), F32)] * 2 + [((devices, LANES), F32)],
        (flags, north8, east8, scale8, *grid, lam),
        scratch=(
            pltpu.VMEM(woven, F32),
            pltpu.VMEM((2, span, LANES), F32),
            pltpu.VMEM((span, LANES), F32),
            pltpu.VMEM(woven, F32),
            pltpu.VMEM(woven, F32),
            pltpu.VMEM((2, span, LANES), F32),
            pltpu.VMEM((span, LANES), F32),
        ),
        flops=10**9,
        nbytes=10**7,
    )
    (both,) = call(pack_kernel, [((slots, 2 * LANES), F32)], (seen, seen_next, ids), nbytes=10**6)
    parts = lax.all_to_all(parts, AXES, split_axis=0, concat_axis=0, tiled=True)
    back, coef = call(
        answer_kernel, [((slots, LANES), F32), ((SUB, LANES), F32)], (parts, both), nbytes=10**6
    )
    back = lax.all_to_all(
        back.reshape(devices, capacity, LANES), AXES, split_axis=0, concat_axis=0, tiled=True
    ).reshape(slots, LANES)
    (increment,) = call(
        increment_kernel,
        [((fields, tile_rows, tile_cols), F32)],
        (image, image_next, coef),
        scratch=(pltpu.VMEM((STEP, span, LANES), F32),),
        nbytes=10**6,
    )
    (departure,) = call(depart_kernel, [((tiles, width), F32)], (back, slot, tables[4], tables[2]))
    return increment, departure


def solution(mesh):
    grid = P(None, "lat", "lon")
    tile = P(AXES, None)
    in_specs = (grid, grid, grid, P("lat", "lon"), P(), tile, tile, tile, P(AXES), tile)
    return jax.shard_map(analyse, mesh=mesh, in_specs=in_specs, out_specs=(grid, tile), check_vma=False)
```
